512 devices in a mesh: crop: 16 (over z, core), dap: 32 (over y, x).
Axes of the slice: x: 4, y: 8, z: 8, core: 2. Of those that a mesh axis runs over, the one named last changes fastest.
Arguments:
- homolog_features: bfloat16 [2048, 128, 256], P(('crop', 'dap')), parts along dimension 0, may hold values from -6 to 6
- twofold_features: bfloat16 [2048, 128, 128], P(('crop', 'dap')), parts along dimension 0, may hold values from -6 to 6
- twofold_offset_map: bfloat16 [128, 8], replicated, may hold values from -0.5 to 0.5
- horizontal_attend_entry_maps: bfloat16 [256, 1024], replicated, may hold values from -2 to 2
- horizontal_attend_exit_map: bfloat16 [256, 256], replicated, may hold values from -0.375 to 0.375
- vertical_attend_entry_maps: bfloat16 [256, 1024], replicated, may hold values from -2 to 2
- vertical_attend_exit_map: bfloat16 [256, 256], replicated, may hold values from -0.375 to 0.375
- tensor_product_factors: bfloat16 [256, 64], replicated, may hold values from -0.375 to 0.375
- tensor_product_exit_map: bfloat16 [1024, 128], replicated, may hold values from -1 to 1
Outputs:
- alignment_output: bfloat16 [2048, 128, 256], P('crop', 'dap'), parts along dimension 0
- pair_output: bfloat16 [2048, 128, 128], P(('crop', 'dap')), parts along dimension 0
The draws below stay inside these ranges and needn't reach their ends.
There are 16 independent parts, one for each index of `crop`. The reference program is written for one: setup_inputs(seed, part) draws one part's arguments, and reference() takes and returns one part's arrays. A program takes and returns all parts, laid end to end along the dimension named above; an argument that names none is the same for every part. Nothing has to cross between parts.
All inputs are finite; a program needn't handle non-finite values.
Results may differ from the reference program's by a relative error of at most 0.0085.
Values may be sent and summed in bfloat16 or wider, within the bound.
A program may use at most 64 MiB of HBM per device.

```python
import math
import jax
import jax.numpy as jnp
from jax import lax

FEATURE_DEPTH = 256
CZ = 128
HEAD_NUMBER = 8
HEAD_DEPTH = 32
PRODUCT_SPAN = 32
HOMOLOG_NUMBER = 128
CROP_LENGTH = 128


def attention_weights(key, random_seed_integer):
    random_samples = jax.random.normal(jax.random.fold_in(key, random_seed_integer), (FEATURE_DEPTH, 4 * HEAD_NUMBER * HEAD_DEPTH), jnp.float32)
    random_samples = jnp.clip(random_samples, -6.0, 6.0) / math.sqrt(FEATURE_DEPTH)
    random_samples = jnp.clip(random_samples, -2.0, 2.0)
    return random_samples.astype(jnp.bfloat16)


def draw_horizontal_attend_entry_maps(key, part):
    return attention_weights(key, 11)


def draw_vertical_attend_entry_maps(key, part):
    return attention_weights(key, 23)


def shard_levels(own_key, dims, cuts, least, high):
    gain = 1.0
    for axis_at, blocks in cuts:
        heights = jax.random.uniform(jax.random.fold_in(jax.random.fold_in(own_key, 6), axis_at), (blocks,), jnp.float32, least / len(cuts), high / len(cuts))
        gain = gain * jnp.repeat(jnp.exp(heights), dims[axis_at] // blocks).reshape((-1,) + (1,) * (len(dims) - 1 - axis_at))
    return gain


def scatter_about(own_key, dims, deviation, most, cuts=(), kind=jnp.bfloat16):
    array = jax.random.normal(own_key, dims, jnp.float32) * deviation
    if len(cuts) > 0:
        array = shard_levels(own_key, dims, cuts, -0.22, 0.18) * array
    return jnp.clip(array, min=-most, max=most).astype(kind)


def setup_inputs(seed: int = 0, part: int = 0) -> dict:
    streams_of = jax.random.split(jax.random.key(seed), 10)
    part_splits = jax.random.split(jax.random.fold_in(streams_of[9], part), 10)
    return {
        "homolog_features": scatter_about(part_splits[0], (HOMOLOG_NUMBER, CROP_LENGTH, FEATURE_DEPTH), 1.0, 6.0, ((0, 32),)),
        "twofold_features": scatter_about(part_splits[1], (CROP_LENGTH, CROP_LENGTH, CZ), 1.0, 6.0, ((0, 32),)),
        "twofold_offset_map": scatter_about(streams_of[2], (CZ, HEAD_NUMBER), CZ ** -0.5, 0.5),
        "horizontal_attend_entry_maps": draw_horizontal_attend_entry_maps(jax.random.fold_in(streams_of[9], 71), part),
        "horizontal_attend_exit_map": scatter_about(streams_of[4], (HEAD_NUMBER * HEAD_DEPTH, FEATURE_DEPTH), (HEAD_NUMBER * HEAD_DEPTH) ** -0.5, 0.375),
        "vertical_attend_entry_maps": draw_vertical_attend_entry_maps(jax.random.fold_in(streams_of[9], 71), part),
        "vertical_attend_exit_map": scatter_about(streams_of[6], (HEAD_NUMBER * HEAD_DEPTH, FEATURE_DEPTH), (HEAD_NUMBER * HEAD_DEPTH) ** -0.5, 0.375),
        "tensor_product_factors": scatter_about(streams_of[7], (FEATURE_DEPTH, 2 * PRODUCT_SPAN), FEATURE_DEPTH ** -0.5, 0.375),
        "tensor_product_exit_map": scatter_about(streams_of[8], (PRODUCT_SPAN * PRODUCT_SPAN, CZ), PRODUCT_SPAN ** -0.5, 1.0),
    }


EPSILON = 1e-05

def standardize_features(values):
    values = values.astype(jnp.float32)
    center = values - lax.optimization_barrier(jnp.mean(values, axis=-1, keepdims=True))
    spread = lax.optimization_barrier(jnp.mean(center * center, axis=-1, keepdims=True))
    return center * lax.rsqrt(spread + EPSILON)

def split_heads(packed, head_count):
    pieces = jnp.split(packed, 4, axis=-1)
    return [piece.reshape(piece.shape[:-1] + (head_count, piece.shape[-1] // head_count)) for piece in pieces]

def attend(queries, key_rows, value_rows, gate_rows, pair_bias):
    head_size = queries.shape[-1]
    scores = jnp.einsum('bihd,bjhd->bhij', queries.astype(jnp.float32), key_rows.astype(jnp.float32)) / math.sqrt(head_size)
    scores = scores + pair_bias
    highest = lax.optimization_barrier(jnp.max(scores, axis=-1, keepdims=True))
    expo = jnp.exp(scores - highest)
    weights = (expo / lax.optimization_barrier(jnp.sum(expo, axis=-1, keepdims=True))).astype(jnp.bfloat16)
    attended = jnp.einsum('bhij,bjhd->bihd', weights.astype(jnp.float32), value_rows.astype(jnp.float32))
    gated = (jax.nn.sigmoid(gate_rows.astype(jnp.float32)) * attended).astype(jnp.bfloat16)
    return gated.reshape(gated.shape[:2] + (gated.shape[2] * gated.shape[3],))

def reference(homolog_features, twofold_features, twofold_offset_map, horizontal_attend_entry_maps, horizontal_attend_exit_map, vertical_attend_entry_maps, vertical_attend_exit_map, tensor_product_factors, tensor_product_exit_map):
    head_count = twofold_offset_map.shape[1]
    horizontal_standardized = standardize_features(homolog_features).astype(jnp.bfloat16)
    horizontal_mapped_features = jnp.einsum('src,cf->srf', horizontal_standardized.astype(jnp.float32), horizontal_attend_entry_maps.astype(jnp.float32)).astype(jnp.bfloat16)
    pair_norm = standardize_features(twofold_features).astype(jnp.bfloat16)
    pair_bias = jnp.einsum('ijz,zh->hij', pair_norm.astype(jnp.float32), twofold_offset_map.astype(jnp.float32)).astype(jnp.bfloat16)
    bias_wide = pair_bias.astype(jnp.float32)[None]
    heads_row = split_heads(horizontal_mapped_features, head_count)

    def one_sequence(items):
        return attend(items[0][None], items[1][None], items[2][None], items[3][None], bias_wide)[0]
    horizontal_sigmoid_scaled = lax.map(one_sequence, tuple(heads_row))
    homolog_line = (homolog_features.astype(jnp.float32) + jnp.einsum('asd,dy->asy', horizontal_sigmoid_scaled.astype(jnp.float32), horizontal_attend_exit_map.astype(jnp.float32))).astype(jnp.bfloat16)
    column_layer_norm = standardize_features(homolog_line).astype(jnp.bfloat16)
    col_proj = jnp.einsum('src,cf->rsf', column_layer_norm.astype(jnp.float32), vertical_attend_entry_maps.astype(jnp.float32)).astype(jnp.bfloat16)
    heads_col = split_heads(col_proj, head_count)

    def one_residue(items):
        return attend(items[0][None], items[1][None], items[2][None], items[3][None], 0.0)[0]
    column_gated_output = lax.map(one_residue, tuple(heads_col))
    alignment_output = (homolog_line.astype(jnp.float32) + jnp.einsum('ihb,by->hiy', column_gated_output.astype(jnp.float32), vertical_attend_exit_map.astype(jnp.float32))).astype(jnp.bfloat16)
    outer_width = tensor_product_factors.shape[1] // 2
    outer_layer_norm = standardize_features(alignment_output).astype(jnp.bfloat16).astype(jnp.float32)
    left = jnp.einsum('src,cf->rsf', outer_layer_norm, tensor_product_factors[:, :outer_width].astype(jnp.float32)).astype(jnp.bfloat16)
    right = jnp.einsum('src,cf->rsf', outer_layer_norm, tensor_product_factors[:, outer_width:].astype(jnp.float32)).astype(jnp.bfloat16)
    right_wide = right.astype(jnp.float32)
    homolog_tally = homolog_features.shape[0]

    def one_row(items):
        left_row, pair_row = items
        product = jnp.einsum('sc,jse->jce', left_row.astype(jnp.float32), right_wide) / homolog_tally
        flat = product.astype(jnp.bfloat16).reshape(product.shape[0], outer_width * outer_width)
        residual_delta = jnp.dot(flat, tensor_product_exit_map, preferred_element_type=jnp.float32)
        return (pair_row.astype(jnp.float32) + residual_delta).astype(jnp.bfloat16)
    pair_output = lax.map(one_row, (left, twofold_features))
    return (alignment_output, pair_output)
```

```python
import math

import jax
import jax.numpy as jnp
from jax import lax
from jax.experimental import pallas as pl
from jax.experimental.pallas import tpu as pltpu
from jax.sharding import PartitionSpec as P

EPSILON = 1e-05
MESH = pl.DeviceIdType.MESH
F32 = jnp.float32
BF16 = jnp.bfloat16
LOG2E = math.log2(math.e)
NX = 4
NY = 8
ND = NX * NY
NT = (((1,), (1,)), ((), ()))


def standardized(values):
    center = values - jnp.mean(values, axis=-1, keepdims=True)
    spread = jnp.mean(center * center, axis=-1, keepdims=True)
    return center * lax.rsqrt(spread + EPSILON)


def dot(a, b):
    return jnp.dot(a, b, preferred_element_type=F32)


def dot_nt(a, b):
    return lax.dot_general(a, b, NT, preferred_element_type=F32)


def put(ref, start, size, value, stride=1):
    rows = pl.ds(start, size, stride=stride) if stride > 1 else pl.ds(start, size)
    for t in range(value.shape[1] // 128):
        ref[t, rows, :] = value[:, t * 128 : (t + 1) * 128]


def take(ref, start, size, stride):
    rows = pl.ds(start, size, stride=stride)
    return jnp.concatenate([ref[t, rows, :] for t in range(ref.shape[0])], axis=1)


def head_masks():
    lane = lax.broadcasted_iota(jnp.int32, (1, 128), 1)
    return [jnp.where(lane // 32 == h, 1.0, 0.0).astype(BF16) for h in range(4)]


def attend(q, k, v, gate, bias, masks):
    scale = LOG2E / math.sqrt(32)
    weights = []
    values = []
    for h in range(4):
        scores = dot_nt(q * masks[h], k) * scale
        if bias is not None:
            scores = scores + bias(h)
        highest = jnp.max(scores, axis=-1, keepdims=True)
        weights.append(jnp.exp2(scores - highest).astype(BF16))
        ones = jnp.broadcast_to(masks[h], v.shape)
        values.append(jnp.concatenate([v * masks[h], ones], axis=1))
    both = dot(jnp.concatenate(weights, axis=1), jnp.concatenate(values, axis=0))
    return (jax.nn.sigmoid(gate) * (both[:, :128] / both[:, 128:])).astype(BF16)


def kernel(
    hom,
    two,
    map_t,
    win,
    wout,
    cwin,
    cwout,
    fac_t,
    tpe,
    align_out,
    pair_out,
    hom_v,
    two_v,
    map_v,
    win_v,
    wout_v,
    cwin_v,
    cwout_v,
    fac_v,
    tpe_v,
    x32,
    n32,
    q_s,
    k_s,
    v_s,
    g_s,
    b32,
    bias_recv,
    bh,
    m32,
    msend,
    mrecv,
    y32,
    align_v,
    l_all,
    r_all,
    o32,
    ot,
    w32,
    bd,
    dsend,
    drecv,
    f32s,
    pair_v,
    in_sem,
    out_sem,
    bs_sem,
    br_sem,
    ms_sem,
    mr_sem,
    ls_sem,
    lr_sem,
    rs_sem,
    rr_sem,
    ds_sem,
    dr_sem,
):
    me = lax.axis_index("dap")
    y = me // NX
    x = lax.rem(me, NX)

    def remote(src, dst, send_sem, recv_sem, target):
        return pltpu.make_async_remote_copy(
            src_ref=src,
            dst_ref=dst,
            send_sem=send_sem,
            recv_sem=recv_sem,
            device_id={"dap": target},
            device_id_type=MESH,
        )

    pairs = [
        (two, two_v),
        (map_t, map_v),
        (hom, hom_v),
        (win, win_v),
        (tpe, tpe_v),
        (wout, wout_v),
        (cwin, cwin_v),
        (cwout, cwout_v),
        (fac_t, fac_v),
    ]
    loads = [pltpu.make_async_copy(a, b, in_sem.at[n]) for n, (a, b) in enumerate(pairs)]
    for load in loads:
        load.start()
    names = ("two", "map", "hom", "win", "tpe", "wout", "cwin", "cwout", "fac")
    ready = dict(zip(names, loads))

    barrier = pltpu.get_barrier_semaphore()

    def greet(step, carry):
        pl.semaphore_signal(
            barrier, inc=1, device_id={"dap": lax.rem(me + step, ND)}, device_id_type=MESH
        )
        return carry

    lax.fori_loop(1, ND, greet, 0)

    ready["two"].wait()
    ready["map"].wait()
    for i in range(4):
        pair_norm = standardized(two_v[i].astype(F32)).astype(BF16)
        b32[pl.ds(i, 8, stride=4), :] = dot_nt(map_v[...], pair_norm)
    bias_recv[me] = b32[0:32, :].astype(BF16)

    pl.semaphore_wait(barrier, ND - 1)

    y_order = [1, 7, 2, 6, 3, 5, 4]
    x_order = [1, 3, 2]
    bias_sends = []

    def send_bias(block, target):
        copy = remote(
            bias_recv.at[block],
            bias_recv.at[block],
            bs_sem.at[len(bias_sends)],
            br_sem.at[block],
            target,
        )
        copy.start()
        bias_sends.append(copy)

    def bias_arrived(block):
        remote(
            bias_recv.at[block], bias_recv.at[block], bs_sem.at[0], br_sem.at[block], me
        ).wait_recv()

    for k in reversed(y_order):
        send_bias(me, lax.rem(y + k, NY) * NX + x)
    for k in reversed(x_order):
        send_bias(me, y * NX + lax.rem(x + k, NX))

    ready["hom"].wait()
    ready["win"].wait()
    masks = head_masks()
    for s in range(4):
        values = hom_v[s].astype(F32)
        put(x32, s * 128, 128, values)
        normal = standardized(values)
        put(n32, s * 128, 128, normal)
        normal = normal.astype(BF16)
        k_s[s] = dot(normal, win_v[:, 256:512]).astype(BF16)
        v_s[s] = dot(normal, win_v[:, 512:768]).astype(BF16)

    def mixed(ref, s):
        return jnp.concatenate(
            [take(ref, s * 128 + i, 32, 4) for i in range(4)], axis=0
        )

    for s in range(4):
        normal = mixed(n32, s).astype(BF16)
        q_s[s] = dot(normal, win_v[:, 0:256]).astype(BF16)
        g_s[s] = dot(normal, win_v[:, 768:1024]).astype(BF16)

    ready["tpe"].wait()
    w32[...] = tpe_v[...].astype(F32)
    bd[...] = jnp.zeros_like(bd)
    for e in range(32):
        piece = w32[pl.ds(e, 32, stride=32), :].astype(BF16)
        for i in range(4):
            bd[e * 128 + i * 32 : e * 128 + (i + 1) * 32, i * 128 : (i + 1) * 128] = piece

    for k in y_order:
        block = lax.rem(y + k, NY) * NX + x
        bias_arrived(block)
        for m in x_order:
            send_bias(block, y * NX + lax.rem(x + m, NX))
    for k in [0] + y_order:
        for m in x_order:
            bias_arrived(lax.rem(y + k, NY) * NX + lax.rem(x + m, NX))

    b32[...] = bias_recv[...].reshape(ND * 32, 128).astype(F32) * LOG2E
    for h in range(8):
        for i in range(4):
            bh[h, i * 32 : (i + 1) * 32, :] = b32[pl.ds(h * 4 + i, 32, stride=32), :]

    ready["wout"].wait()
    for s in range(4):
        gated = []
        for g in range(2):
            lanes = slice(g * 128, (g + 1) * 128)
            gated.append(
                attend(
                    q_s[s, :, lanes],
                    k_s[s, :, lanes],
                    v_s[s, :, lanes],
                    g_s[s, :, lanes].astype(F32),
                    lambda h: bh[g * 4 + h],
                    masks,
                )
            )
        total = mixed(x32, s) + dot(jnp.concatenate(gated, axis=1), wout_v[...])
        put(m32, s * 128, 128, total)

    for d in range(ND):
        msend[d] = take(m32, d, 16, ND).astype(BF16)

    mrecv[me] = msend[me]

    def send_rows(step, carry):
        target = lax.rem(me + step, ND)
        remote(msend.at[target], mrecv.at[me], ms_sem, mr_sem, target).start()
        return carry

    lax.fori_loop(1, ND, send_rows, 0)

    for copy in bias_sends:
        copy.wait_send()
    for name in ("cwin", "cwout", "fac"):
        ready[name].wait()

    others = remote(
        msend.at[pl.ds(0, ND - 1)], mrecv.at[pl.ds(0, ND - 1)], ms_sem, mr_sem, me
    )
    others.wait_recv()
    others.wait_send()

    put(x32, 0, ND * 16, mrecv[...].reshape(ND * 16, 256).astype(F32))
    for r in range(4):
        values = take(x32, r, 128, 4)
        normal = standardized(values).astype(BF16)
        packed = [dot(normal, cwin_v[:, n * 256 : (n + 1) * 256]).astype(BF16) for n in range(4)]
        gated = []
        for g in range(2):
            lanes = slice(g * 128, (g + 1) * 128)
            q, k, v, gate = [part[:, lanes] for part in packed]
            gated.append(attend(q, k, v, gate.astype(F32), None, masks))
        total = (values + dot(jnp.concatenate(gated, axis=1), cwout_v[...])).astype(BF16)
        wide = total.astype(F32)
        put(y32, r, 128, wide, stride=4)
        outer_norm = standardized(wide).astype(BF16)
        factors = dot_nt(fac_v[...], outer_norm).astype(BF16)
        l_all[x, r * 32 : (r + 1) * 32, :] = factors[:32]
        r_all[y, r * 32 : (r + 1) * 32, :] = factors[32:]

    sends = []
    for n, k in enumerate(reversed(y_order)):
        target = lax.rem(y + k, NY) * NX + x
        sends.append(remote(r_all.at[y], r_all.at[y], rs_sem.at[n], rr_sem.at[y], target))
    for n, k in enumerate(reversed(x_order)):
        target = y * NX + lax.rem(x + k, NX)
        sends.append(remote(l_all.at[x], l_all.at[x], ls_sem.at[n], lr_sem.at[x], target))
    for copy in sends:
        copy.start()

    align_v[...] = jnp.concatenate([y32[0], y32[1]], axis=1).astype(BF16)
    align_store = pltpu.make_async_copy(align_v, align_out, out_sem.at[0])
    align_store.start()

    for k in x_order:
        peer = lax.rem(x + k, NX)
        remote(l_all.at[peer], l_all.at[peer], ls_sem.at[0], lr_sem.at[peer], me).wait_recv()
    left = l_all[...].reshape(NX * 128, 128)
    for k in [0] + y_order:
        peer = lax.rem(y + k, NY)
        if k:
            remote(r_all.at[peer], r_all.at[peer], rs_sem.at[0], rr_sem.at[peer], me).wait_recv()
        product = dot_nt(r_all[peer], left) * (1.0 / 128)
        put(o32, pl.multiple_of(peer * 128, 128), 128, product)
    for e in range(32):
        ot[:, e * 128 : (e + 1) * 128] = jnp.concatenate(
            [
                o32[n, pl.ds(j * 32 + e, 8, stride=128), :]
                for n in range(NX)
                for j in range(4)
            ],
            axis=0,
        ).astype(BF16)
    dsend[...] = dot(ot[...], bd[...]).astype(BF16).reshape(NX, 32, 512)
    drecv[x] = dsend[x]
    for n, k in enumerate(x_order):
        peer = lax.rem(x + k, NX)
        copy = remote(
            dsend.at[peer], drecv.at[x], ds_sem.at[n], dr_sem.at[x], y * NX + peer
        )
        copy.start()
        sends.append(copy)
    for k in x_order:
        peer = lax.rem(x + k, NX)
        remote(dsend.at[peer], drecv.at[peer], ds_sem.at[0], dr_sem.at[peer], me).wait_recv()
    for n in range(NX):
        block = drecv[n].astype(F32)
        for i in range(4):
            for j in range(4):
                f32s[pl.ds(i * 128 + n * 4 + j, 8, stride=16), :] = block[
                    j * 8 : (j + 1) * 8, i * 128 : (i + 1) * 128
                ]
    pair_v[...] = (f32s[...] + two_v[...].reshape(512, 128).astype(F32)).astype(BF16).reshape(4, 128, 128)
    pair_store = pltpu.make_async_copy(pair_v, pair_out, out_sem.at[1])
    pair_store.start()
    for copy in sends:
        copy.wait_send()
    align_store.wait()
    pair_store.wait()


def per_device(hom, two, offset_map, win, wout, cwin, cwout, factors, tpe):
    operands = (hom, two, offset_map.T, win, wout, cwin, cwout, factors.T, tpe)
    dma = pltpu.SemaphoreType.DMA
    vm = pltpu.VMEM
    scratch = [vm(a.shape, BF16) for a in operands] + [
        vm((2, 512, 128), F32),
        vm((2, 512, 128), F32),
        vm((4, 128, 256), BF16),
        vm((4, 128, 256), BF16),
        vm((4, 128, 256), BF16),
        vm((4, 128, 256), BF16),
        vm((ND * 32, 128), F32),
        vm((ND, 32, 128), BF16),
        vm((8, 128, 128), F32),
        vm((2, 512, 128), F32),
        vm((ND, 16, 256), BF16),
        vm((ND, 16, 256), BF16),
        vm((2, 512, 128), F32),
        vm((512, 256), BF16),
        vm((NX, 128, 128), BF16),
        vm((NY, 128, 128), BF16),
        vm((NX, NY * 128, 128), F32),
        vm((128, 4096), BF16),
        vm((1024, 128), F32),
        vm((4096, 512), BF16),
        vm((NX, 32, 512), BF16),
        vm((NX, 32, 512), BF16),
        vm((512, 128), F32),
        vm((4, 128, 128), BF16),
        dma((9,)),
        dma((2,)),
        dma((31,)),
        dma((ND,)),
        dma,
        dma,
        dma((3,)),
        dma((NX,)),
        dma((7,)),
        dma((NY,)),
        dma((3,)),
        dma((NX,)),
    ]
    hbm = pl.BlockSpec(memory_space=pl.ANY)
    align, pair = pl.pallas_call(
        kernel,
        out_shape=(
            jax.ShapeDtypeStruct((512, 256), BF16),
            jax.ShapeDtypeStruct((4, 128, 128), BF16),
        ),
        in_specs=[hbm] * len(operands),
        out_specs=(hbm, hbm),
        scratch_shapes=scratch,
        compiler_params=pltpu.CompilerParams(collective_id=0, has_side_effects=True),
    )(*operands)
    return align.reshape(128, 4, 256), pair


def solution(mesh):
    split = P(("crop", "dap"), None, None)
    return jax.shard_map(
        per_device,
        mesh=mesh,
        in_specs=(split, split) + (P(),) * 7,
        out_specs=(P("crop", "dap", None), split),
        check_vma=False,
    )
```

```python
import math

import jax
import jax.numpy as jnp
from jax import lax
from jax.experimental import pallas as pl
from jax.experimental.pallas import tpu as pltpu
from jax.sharding import PartitionSpec as P

EPSILON = 1e-05
MESH = pl.DeviceIdType.MESH
F32 = jnp.float32
BF16 = jnp.bfloat16
LOG2E = math.log2(math.e)
NX = 4
NY = 8
ND = NX * NY
NT = (((1,), (1,)), ((), ()))


def standardized(values):
    center = values - jnp.mean(values, axis=-1, keepdims=True)
    spread = jnp.mean(center * center, axis=-1, keepdims=True)
    return center * lax.rsqrt(spread + EPSILON)


def dot(a, b):
    return jnp.dot(a, b, preferred_element_type=F32)


def dot_nt(a, b):
    return lax.dot_general(a, b, NT, preferred_element_type=F32)


def put(ref, start, size, value, stride=1):
    rows = pl.ds(start, size, stride=stride) if stride > 1 else pl.ds(start, size)
    for t in range(value.shape[1] // 128):
        ref[t, rows, :] = value[:, t * 128 : (t + 1) * 128]


def take(ref, start, size, stride):
    rows = pl.ds(start, size, stride=stride)
    return jnp.concatenate([ref[t, rows, :] for t in range(ref.shape[0])], axis=1)


def head_masks():
    lane = lax.broadcasted_iota(jnp.int32, (1, 128), 1)
    return [jnp.where(lane // 32 == h, 1.0, 0.0).astype(BF16) for h in range(4)]


def attend(q, k, v, gate, masks):
    scale = LOG2E / math.sqrt(32)
    weights = []
    values = []
    for h in range(4):
        scores = dot_nt(q * masks[h], k) * scale
        highest = jnp.max(scores, axis=-1, keepdims=True)
        weights.append(jnp.exp2(scores - highest).astype(BF16))
        ones = jnp.broadcast_to(masks[h], v.shape)
        values.append(jnp.concatenate([v * masks[h], ones], axis=1))
    both = dot(jnp.concatenate(weights, axis=1), jnp.concatenate(values, axis=0))
    return (jax.nn.sigmoid(gate) * (both[:, :128] / both[:, 128:])).astype(BF16)


def kernel(
    hom,
    two,
    map_t,
    win,
    wout,
    cwin,
    cwout,
    fac_t,
    tpe,
    align_out,
    pair_out,
    hom_v,
    two_v,
    map_v,
    win_v,
    wout_v,
    cwin_v,
    cwout_v,
    fac_v,
    tpe_v,
    x32,
    n32,
    q_s,
    k_s,
    v_s,
    g_s,
    xp,
    b32,
    bias_recv,
    m32,
    msend,
    mrecv,
    y32,
    align_v,
    l_all,
    r_all,
    o32,
    ot,
    w32,
    bd,
    dsend,
    drecv,
    f32s,
    pair_v,
    in_sem,
    out_sem,
    bs_sem,
    br_sem,
    ms_sem,
    mr_sem,
    ls_sem,
    lr_sem,
    rs_sem,
    rr_sem,
    ds_sem,
    dr_sem,
):
    me = lax.axis_index("dap")
    y = me // NX
    x = lax.rem(me, NX)

    def remote(src, dst, send_sem, recv_sem, target):
        return pltpu.make_async_remote_copy(
            src_ref=src,
            dst_ref=dst,
            send_sem=send_sem,
            recv_sem=recv_sem,
            device_id={"dap": target},
            device_id_type=MESH,
        )

    pairs = [
        (two, two_v),
        (map_t, map_v),
        (hom, hom_v),
        (win, win_v),
        (tpe, tpe_v),
        (wout, wout_v),
        (cwin, cwin_v),
        (cwout, cwout_v),
        (fac_t, fac_v),
    ]
    loads = [pltpu.make_async_copy(a, b, in_sem.at[n]) for n, (a, b) in enumerate(pairs)]
    for load in loads:
        load.start()
    names = ("two", "map", "hom", "win", "tpe", "wout", "cwin", "cwout", "fac")
    ready = dict(zip(names, loads))

    barrier = pltpu.get_barrier_semaphore()

    y_order = [1, 7, 2, 6, 3, 5, 4]
    x_order = [1, 3, 2]

    def at(dy, dx):
        return lax.rem(y + dy, NY) * NX + lax.rem(x + dx, NX)

    for dy, dx in [(k, 0) for k in reversed(y_order)] + [(0, k) for k in reversed(x_order)]:
        pl.semaphore_signal(barrier, inc=1, device_id={"dap": at(dy, dx)}, device_id_type=MESH)

    ready["two"].wait()
    ready["map"].wait()
    for i in range(4):
        pair_norm = standardized(two_v[i].astype(F32)).astype(BF16)
        b32[0, pl.ds(i, 8, stride=4), :] = dot_nt(map_v[...], pair_norm)
    bias_recv[me] = b32[0, 0:32, :].astype(BF16)

    pl.semaphore_wait(barrier, NY + NX - 2)

    bias_sends = []

    def send_bias(block, target):
        copy = remote(
            bias_recv.at[block],
            bias_recv.at[block],
            bs_sem.at[len(bias_sends)],
            br_sem.at[block],
            target,
        )
        copy.start()
        bias_sends.append(copy)

    def bias_arrived(block):
        remote(
            bias_recv.at[block], bias_recv.at[block], bs_sem.at[0], br_sem.at[block], me
        ).wait_recv()

    for k in reversed(y_order):
        send_bias(me, at(k, 0))
    for k in reversed(x_order):
        send_bias(me, at(0, k))

    ready["hom"].wait()
    ready["win"].wait()
    masks = head_masks()
    wide_masks = [jnp.concatenate([mask, mask], axis=1).astype(F32) for mask in masks]
    values = hom_v[...].reshape(512, 256).astype(F32)
    put(x32, 0, 512, values)
    normal = standardized(values)
    put(n32, 0, 512, normal)
    normal = normal.astype(BF16)
    k_s[...] = dot(normal, win_v[:, 256:512]).astype(BF16)
    v_s[...] = dot(normal, win_v[:, 512:768]).astype(BF16)

    def mixed(ref, group):
        return jnp.concatenate(
            [take(ref, s * 128 + group * 4 + i, 8, 16) for s in range(4) for i in range(4)],
            axis=0,
        )

    normal = jnp.concatenate([mixed(n32, group) for group in range(NX)], axis=0).astype(BF16)
    q_s[...] = dot(normal, win_v[:, 0:256]).astype(BF16).reshape(NX, 128, 256)
    gates = dot(normal, win_v[:, 768:1024]).astype(BF16).astype(F32)
    g_s[...] = jax.nn.sigmoid(gates).reshape(NX, 128, 256)
    for group in range(NX):
        xp[group] = mixed(x32, group)

    ready["tpe"].wait()
    w32[...] = tpe_v[...].astype(F32)
    bd[...] = jnp.zeros_like(bd)
    for e in range(32):
        piece = w32[pl.ds(e, 32, stride=32), :].astype(BF16)
        for i in range(4):
            bd[e * 128 + i * 32 : e * 128 + (i + 1) * 32, i * 128 : (i + 1) * 128] = piece

    for k in y_order:
        block = at(k, 0)
        bias_arrived(block)
        for m in reversed(x_order):
            send_bias(block, at(0, m))

    ready["wout"].wait()
    scale = LOG2E / math.sqrt(32)
    ones = jnp.ones((128, 128), BF16)
    for n, m in enumerate([0] + x_order):
        column = lax.rem(x + m, NX)
        if m:
            for k in [0] + y_order:
                bias_arrived(at(k, m))
        for r in range(NY):
            b32[n, r * 32 : (r + 1) * 32, :] = bias_recv[r * NX + column].astype(F32) * LOG2E
        bias = [
            jnp.concatenate(
                [b32[n, pl.ds(g * 16 + i, 8, stride=32), :] for i in range(16)], axis=0
            )
            for g in range(2)
        ]
        parts = []
        for g in range(2):
            lanes = slice(g * 128, (g + 1) * 128)
            part = []
            for s in range(4):
                rows = slice(s * 32, (s + 1) * 32)
                query = q_s[column, rows, lanes]
                query = jnp.concatenate([query * mask for mask in masks], axis=0)
                scores = dot_nt(query, k_s[s * 128 : (s + 1) * 128, lanes]) * scale + bias[g]
                highest = jnp.max(scores, axis=-1, keepdims=True)
                weights = jnp.exp2(scores - highest).astype(BF16)
                value = jnp.concatenate([v_s[s * 128 : (s + 1) * 128, lanes], ones], axis=1)
                both = dot(weights, value)
                both = sum(
                    both[h * 32 : (h + 1) * 32] * wide_masks[h] for h in range(4)
                )
                part.append(both[:, :128] / both[:, 128:] * g_s[column, rows, lanes])
            parts.append(jnp.concatenate(part, axis=0).astype(BF16))
        total = xp[column] + dot(jnp.concatenate(parts, axis=1), wout_v[...])
        put(m32.at[n], 0, 128, total)
        for r in range(NY):
            msend[r * NX + column] = take(m32.at[n], r, 16, 8).astype(BF16)
        if not m:
            mrecv[me] = msend[me]
        for k in ([] if m == 0 else [0]) + y_order:
            target = at(k, m)
            remote(msend.at[target], mrecv.at[me], ms_sem, mr_sem, target).start()

    for copy in bias_sends:
        copy.wait_send()
    for name in ("cwin", "cwout", "fac"):
        ready[name].wait()

    others = remote(
        msend.at[pl.ds(0, ND - 1)], mrecv.at[pl.ds(0, ND - 1)], ms_sem, mr_sem, me
    )
    others.wait_recv()
    others.wait_send()

    put(x32, 0, ND * 16, mrecv[...].reshape(ND * 16, 256).astype(F32))
    sends = []
    for half in range(2):
        pair = (half * 2, half * 2 + 1)
        values = jnp.concatenate([take(x32, r, 128, 4) for r in pair], axis=0)
        normal = standardized(values).astype(BF16)
        packed = [dot(normal, cwin_v[:, n * 256 : (n + 1) * 256]).astype(BF16) for n in range(4)]
        gated = []
        for n in range(2):
            parts = []
            for g in range(2):
                q, k, v, gate = [
                    part[n * 128 : (n + 1) * 128, g * 128 : (g + 1) * 128] for part in packed
                ]
                parts.append(attend(q, k, v, gate.astype(F32), masks))
            gated.append(jnp.concatenate(parts, axis=1))
        total = values + dot(jnp.concatenate(gated, axis=0), cwout_v[...])
        wide = total.astype(BF16).astype(F32)
        factors = dot_nt(fac_v[...], standardized(wide).astype(BF16)).astype(BF16)
        for n, r in enumerate(pair):
            l_all[x, r * 32 : (r + 1) * 32, :] = factors[:32, n * 128 : (n + 1) * 128]
            r_all[y, r * 32 : (r + 1) * 32, :] = factors[32:, n * 128 : (n + 1) * 128]
        for n, r in enumerate(pair):
            put(y32, r, 128, wide[n * 128 : (n + 1) * 128], stride=4)
        rows = pl.ds(half * 64, 64)
        start = len(sends)
        for n, k in enumerate(reversed(y_order)):
            block = r_all.at[y, rows]
            sends.append(
                remote(block, block, rs_sem.at[half, n], rr_sem.at[half, y], at(k, 0))
            )
        for n, k in enumerate(reversed(x_order)):
            block = l_all.at[x, rows]
            sends.append(
                remote(block, block, ls_sem.at[half, n], lr_sem.at[half, x], at(0, k))
            )
        for copy in sends[start:]:
            copy.start()

    align_v[...] = jnp.concatenate([y32[0], y32[1]], axis=1).reshape(128, 4, 256).astype(BF16)
    align_store = pltpu.make_async_copy(align_v, align_out, out_sem.at[0])
    align_store.start()

    def arrived(ref, peer, send_sem, recv_sem):
        for half in range(2):
            block = ref.at[peer, pl.ds(half * 64, 64)]
            remote(block, block, send_sem.at[half, 0], recv_sem.at[half, peer], me).wait_recv()

    for k in x_order:
        arrived(l_all, lax.rem(x + k, NX), ls_sem, lr_sem)
    left = l_all[...].reshape(NX * 128, 128)
    for k in [0] + y_order:
        peer = lax.rem(y + k, NY)
        if k:
            arrived(r_all, peer, rs_sem, rr_sem)
        product = dot_nt(r_all[peer], left) * (1.0 / 128)
        put(o32, pl.multiple_of(peer * 128, 128), 128, product)
    for e in range(32):
        ot[:, e * 128 : (e + 1) * 128] = jnp.concatenate(
            [
                o32[n, pl.ds(j * 32 + e, 8, stride=128), :]
                for n in range(NX)
                for j in range(4)
            ],
            axis=0,
        ).astype(BF16)
    for half in range(2):
        product = dot(ot[...], bd[:, half * 256 : (half + 1) * 256])
        dsend[half] = product.astype(BF16).reshape(NX, 32, 256)
        for n, k in enumerate(reversed(x_order)):
            peer = lax.rem(x + k, NX)
            copy = remote(
                dsend.at[half, peer],
                drecv.at[half, x],
                ds_sem.at[half, n],
                dr_sem.at[half, x],
                at(0, k),
            )
            copy.start()
            sends.append(copy)
    drecv[:, x] = dsend[:, x]
    for k in [0] + x_order:
        peer = lax.rem(x + k, NX)
        for half in range(2):
            if k:
                block = drecv.at[half, peer]
                remote(
                    block, block, ds_sem.at[half, 0], dr_sem.at[half, peer], me
                ).wait_recv()
            block = drecv[half, peer].astype(F32)
            for i in range(2):
                for j in range(4):
                    f32s[pl.ds((half * 2 + i) * 128 + peer * 4 + j, 8, stride=16), :] = block[
                        j * 8 : (j + 1) * 8, i * 128 : (i + 1) * 128
                    ]
    pair_v[...] = (f32s[...] + two_v[...].reshape(512, 128).astype(F32)).astype(BF16).reshape(4, 128, 128)
    pair_store = pltpu.make_async_copy(pair_v, pair_out, out_sem.at[1])
    pair_store.start()
    for copy in sends:
        copy.wait_send()
    align_store.wait()
    pair_store.wait()


def per_device(hom, two, offset_map, win, wout, cwin, cwout, factors, tpe):
    operands = (hom, two, offset_map.T, win, wout, cwin, cwout, factors.T, tpe)
    dma = pltpu.SemaphoreType.DMA
    vm = pltpu.VMEM
    scratch = [vm(a.shape, BF16) for a in operands] + [
        vm((2, 512, 128), F32),
        vm((2, 512, 128), F32),
        vm((NX, 128, 256), BF16),
        vm((512, 256), BF16),
        vm((512, 256), BF16),
        vm((NX, 128, 256), F32),
        vm((NX, 128, 256), F32),
        vm((NX, 256, 128), F32),
        vm((ND, 32, 128), BF16),
        vm((NX, 2, 128, 128), F32),
        vm((ND, 16, 256), BF16),
        vm((ND, 16, 256), BF16),
        vm((2, 512, 128), F32),
        vm((128, 4, 256), BF16),
        vm((NX, 128, 128), BF16),
        vm((NY, 128, 128), BF16),
        vm((NX, NY * 128, 128), F32),
        vm((128, 4096), BF16),
        vm((1024, 128), F32),
        vm((4096, 512), BF16),
        vm((2, NX, 32, 256), BF16),
        vm((2, NX, 32, 256), BF16),
        vm((512, 128), F32),
        vm((4, 128, 128), BF16),
        dma((9,)),
        dma((2,)),
        dma((31,)),
        dma((ND,)),
        dma,
        dma,
        dma((2, 3)),
        dma((2, NX)),
        dma((2, 7)),
        dma((2, NY)),
        dma((2, 3)),
        dma((2, NX)),
    ]
    hbm = pl.BlockSpec(memory_space=pl.ANY)
    align, pair = pl.pallas_call(
        kernel,
        out_shape=(
            jax.ShapeDtypeStruct((128, 4, 256), BF16),
            jax.ShapeDtypeStruct((4, 128, 128), BF16),
        ),
        in_specs=[hbm] * len(operands),
        out_specs=(hbm, hbm),
        scratch_shapes=scratch,
        compiler_params=pltpu.CompilerParams(collective_id=0, has_side_effects=True),
    )(*operands)
    return align, pair


def solution(mesh):
    split = P(("crop", "dap"), None, None)
    return jax.shard_map(
        per_device,
        mesh=mesh,
        in_specs=(split, split) + (P(),) * 7,
        out_specs=(P("crop", "dap", None), split),
        check_vma=False,
    )
```

```python
import math

import jax
import jax.numpy as jnp
from jax import lax
from jax.experimental import pallas as pl
from jax.experimental.pallas import tpu as pltpu
from jax.sharding import PartitionSpec as P

EPSILON = 1e-05
MESH = pl.DeviceIdType.MESH
F32 = jnp.float32
BF16 = jnp.bfloat16
LOG2E = math.log2(math.e)
NX = 4
NY = 8
ND = NX * NY
NT = (((1,), (1,)), ((), ()))


def standardized(values):
    center = values - jnp.mean(values, axis=-1, keepdims=True)
    spread = jnp.mean(center * center, axis=-1, keepdims=True)
    return center * lax.rsqrt(spread + EPSILON)


def dot(a, b):
    return jnp.dot(a, b, preferred_element_type=F32)


def dot_nt(a, b):
    return lax.dot_general(a, b, NT, preferred_element_type=F32)


def put(ref, start, size, value, stride=1):
    rows = pl.ds(start, size, stride=stride) if stride > 1 else pl.ds(start, size)
    for t in range(value.shape[1] // 128):
        ref[t, rows, :] = value[:, t * 128 : (t + 1) * 128]


def take(ref, start, size, stride):
    rows = pl.ds(start, size, stride=stride)
    return jnp.concatenate([ref[t, rows, :] for t in range(ref.shape[0])], axis=1)


def head_masks():
    lane = lax.broadcasted_iota(jnp.int32, (1, 128), 1)
    return [jnp.where(lane // 32 == h, 1.0, 0.0).astype(BF16) for h in range(4)]


def attend(q, k, v, gate, masks):
    scale = LOG2E / math.sqrt(32)
    weights = []
    values = []
    for h in range(4):
        scores = dot_nt(q * masks[h], k) * scale
        highest = jnp.max(scores, axis=-1, keepdims=True)
        weights.append(jnp.exp2(scores - highest).astype(BF16))
        ones = jnp.broadcast_to(masks[h], v.shape)
        values.append(jnp.concatenate([v * masks[h], ones], axis=1))
    both = dot(jnp.concatenate(weights, axis=1), jnp.concatenate(values, axis=0))
    return (jax.nn.sigmoid(gate) * (both[:, :128] / both[:, 128:])).astype(BF16)


def kernel(
    hom,
    two,
    map_t,
    win,
    wout,
    cwin,
    cwout,
    fac_t,
    tpe,
    align_out,
    pair_out,
    hom_v,
    two_v,
    map_v,
    win_v,
    wout_v,
    cwin_v,
    cwout_v,
    fac_v,
    tpe_v,
    x32,
    n32,
    q_s,
    k_s,
    v_s,
    g_s,
    xp,
    b32,
    bias_recv,
    m32,
    msend,
    mrecv,
    y32,
    l_all,
    r_all,
    o32,
    ot,
    w32,
    bd,
    dsend,
    drecv,
    f32s,
    in_sem,
    bs_sem,
    br_sem,
    ms_sem,
    mr_sem,
    ls_sem,
    lr_sem,
    rs_sem,
    rr_sem,
    ds_sem,
    dr_sem,
):
    me = lax.axis_index("dap")
    y = me // NX
    x = lax.rem(me, NX)

    def remote(src, dst, send_sem, recv_sem, target):
        return pltpu.make_async_remote_copy(
            src_ref=src,
            dst_ref=dst,
            send_sem=send_sem,
            recv_sem=recv_sem,
            device_id={"dap": target},
            device_id_type=MESH,
        )

    pairs = [
        (two, two_v),
        (map_t, map_v),
        (hom, hom_v),
        (win, win_v),
        (tpe, tpe_v),
        (wout, wout_v),
        (cwin, cwin_v),
        (cwout, cwout_v),
        (fac_t, fac_v),
    ]
    loads = [pltpu.make_async_copy(a, b, in_sem.at[n]) for n, (a, b) in enumerate(pairs)]
    for load in loads:
        load.start()
    names = ("two", "map", "hom", "win", "tpe", "wout", "cwin", "cwout", "fac")
    ready = dict(zip(names, loads))

    barrier = pltpu.get_barrier_semaphore()

    y_order = [1, 7, 2, 6, 3, 5, 4]
    x_order = [1, 3, 2]

    def at(dy, dx):
        return lax.rem(y + dy, NY) * NX + lax.rem(x + dx, NX)

    for dy, dx in [(k, 0) for k in reversed(y_order)] + [(0, k) for k in reversed(x_order)]:
        pl.semaphore_signal(barrier, inc=1, device_id={"dap": at(dy, dx)}, device_id_type=MESH)

    ready["two"].wait()
    ready["map"].wait()
    for i in range(4):
        pair_norm = standardized(two_v[i].astype(F32)).astype(BF16)
        b32[0, pl.ds(i, 8, stride=4), :] = dot_nt(map_v[...], pair_norm)
    bias_recv[me] = b32[0, 0:32, :].astype(BF16)

    pl.semaphore_wait(barrier, NY + NX - 2)

    bias_sends = []

    def send_bias(block, target):
        copy = remote(
            bias_recv.at[block],
            bias_recv.at[block],
            bs_sem.at[len(bias_sends)],
            br_sem.at[block],
            target,
        )
        copy.start()
        bias_sends.append(copy)

    def bias_arrived(block):
        remote(
            bias_recv.at[block], bias_recv.at[block], bs_sem.at[0], br_sem.at[block], me
        ).wait_recv()

    for k in reversed(y_order):
        send_bias(me, at(k, 0))
    for k in reversed(x_order):
        send_bias(me, at(0, k))

    ready["hom"].wait()
    ready["win"].wait()
    masks = head_masks()
    wide_masks = [jnp.concatenate([mask, mask], axis=1).astype(F32) for mask in masks]
    values = hom_v[...].reshape(512, 256).astype(F32)
    put(x32, 0, 512, values)
    normal = standardized(values)
    put(n32, 0, 512, normal)
    normal = normal.astype(BF16)
    k_s[...] = dot(normal, win_v[:, 256:512]).astype(BF16)
    v_s[...] = dot(normal, win_v[:, 512:768]).astype(BF16)

    def mixed(ref, group):
        return jnp.concatenate(
            [take(ref, s * 128 + group * 4 + i, 8, 16) for s in range(4) for i in range(4)],
            axis=0,
        )

    normal = jnp.concatenate([mixed(n32, group) for group in range(NX)], axis=0).astype(BF16)
    q_s[...] = dot(normal, win_v[:, 0:256]).astype(BF16).reshape(NX, 128, 256)
    gates = dot(normal, win_v[:, 768:1024]).astype(BF16).astype(F32)
    g_s[...] = jax.nn.sigmoid(gates).reshape(NX, 128, 256)
    for group in range(NX):
        xp[group] = mixed(x32, group)

    ready["tpe"].wait()
    w32[...] = tpe_v[...].astype(F32)
    bd[...] = jnp.zeros_like(bd)
    for e in range(32):
        piece = w32[pl.ds(e, 32, stride=32), :].astype(BF16)
        for i in range(4):
            bd[e * 128 + i * 32 : e * 128 + (i + 1) * 32, i * 128 : (i + 1) * 128] = piece

    for k in y_order:
        block = at(k, 0)
        bias_arrived(block)
        for m in reversed(x_order):
            send_bias(block, at(0, m))

    ready["wout"].wait()
    scale = LOG2E / math.sqrt(32)
    ones = jnp.ones((128, 128), BF16)
    for n, m in enumerate([0, 1, 2, 3]):
        column = lax.rem(x + m, NX)
        if m:
            for k in [0] + y_order:
                bias_arrived(at(k, m))
        for r in range(NY):
            b32[n, r * 32 : (r + 1) * 32, :] = bias_recv[r * NX + column].astype(F32) * LOG2E
        bias = [
            jnp.concatenate(
                [b32[n, pl.ds(g * 16 + i, 8, stride=32), :] for i in range(16)], axis=0
            )
            for g in range(2)
        ]
        parts = []
        for g in range(2):
            lanes = slice(g * 128, (g + 1) * 128)
            part = []
            for s in range(4):
                rows = slice(s * 32, (s + 1) * 32)
                query = q_s[column, rows, lanes]
                query = jnp.concatenate([query * mask for mask in masks], axis=0)
                scores = dot_nt(query, k_s[s * 128 : (s + 1) * 128, lanes]) * scale + bias[g]
                highest = jnp.max(scores, axis=-1, keepdims=True)
                weights = jnp.exp2(scores - highest).astype(BF16)
                value = jnp.concatenate([v_s[s * 128 : (s + 1) * 128, lanes], ones], axis=1)
                both = dot(weights, value)
                both = sum(
                    both[h * 32 : (h + 1) * 32] * wide_masks[h] for h in range(4)
                )
                part.append(both[:, :128] / both[:, 128:] * g_s[column, rows, lanes])
            parts.append(jnp.concatenate(part, axis=0).astype(BF16))
        total = xp[column] + dot(jnp.concatenate(parts, axis=1), wout_v[...])
        for s in range(4):
            for i in range(4):
                start = s * 32 + i * 8
                for t in range(2):
                    m32[n, t, pl.ds(i * 4 + s, 8, stride=16), :] = total[
                        start : start + 8, t * 128 : (t + 1) * 128
                    ]
        for r in range(NY):
            rows = slice(r * 16, (r + 1) * 16)
            msend[r * NX + column] = jnp.concatenate(
                [m32[n, 0, rows, :], m32[n, 1, rows, :]], axis=1
            ).astype(BF16)
        if not m:
            mrecv[me] = msend[me]
        for k in list(reversed(y_order)) + ([] if m == 0 else [0]):
            target = at(k, m)
            remote(msend.at[target], mrecv.at[me], ms_sem, mr_sem.at[m], target).start()

    for copy in bias_sends:
        copy.wait_send()
    for name in ("cwin", "cwout", "fac"):
        ready[name].wait()

    for m in range(NX):
        column = lax.rem(x + NX - m, NX)
        count = NY - 1 if m == 0 else NY
        group = mrecv.at[pl.ds(0, count)]
        remote(group, group, ms_sem, mr_sem.at[m], me).wait_recv()
        values = jnp.concatenate([mrecv[r * NX + column] for r in range(NY)], axis=0).astype(F32)
        normal = standardized(values)
        base = pl.multiple_of(column * 32, 32)
        for r in range(NY):
            for i in range(4):
                start = r * 16 + i * 4
                for t in range(2):
                    lanes = slice(t * 128, (t + 1) * 128)
                    x32.at[t, pl.ds(i * 128 + base, 32), :][r * 4 : (r + 1) * 4, :] = values[
                        start : start + 4, lanes
                    ]
                    n32.at[t, pl.ds(i * 128 + base, 32), :][r * 4 : (r + 1) * 4, :] = normal[
                        start : start + 4, lanes
                    ]
    everything = msend.at[pl.ds(0, ND - 1)]
    remote(everything, everything, ms_sem, mr_sem.at[0], me).wait_send()

    sends = []
    for half in range(2):
        pair = (half * 2, half * 2 + 1)
        rows = slice(half * 256, (half + 1) * 256)
        values = jnp.concatenate([x32[0, rows, :], x32[1, rows, :]], axis=1)
        normal = jnp.concatenate([n32[0, rows, :], n32[1, rows, :]], axis=1).astype(BF16)
        packed = [dot(normal, cwin_v[:, n * 256 : (n + 1) * 256]).astype(BF16) for n in range(4)]
        gated = []
        for n in range(2):
            parts = []
            for g in range(2):
                q, k, v, gate = [
                    part[n * 128 : (n + 1) * 128, g * 128 : (g + 1) * 128] for part in packed
                ]
                parts.append(attend(q, k, v, gate.astype(F32), masks))
            gated.append(jnp.concatenate(parts, axis=1))
        total = values + dot(jnp.concatenate(gated, axis=0), cwout_v[...])
        wide = total.astype(BF16).astype(F32)
        factors = dot_nt(fac_v[...], standardized(wide).astype(BF16)).astype(BF16)
        for n, r in enumerate(pair):
            l_all[x, r * 32 : (r + 1) * 32, :] = factors[:32, n * 128 : (n + 1) * 128]
            r_all[y, r * 32 : (r + 1) * 32, :] = factors[32:, n * 128 : (n + 1) * 128]
        rows = pl.ds(half * 64, 64)
        start = len(sends)
        for n, k in enumerate(reversed(y_order)):
            block = r_all.at[y, rows]
            sends.append(
                remote(block, block, rs_sem.at[half, n], rr_sem.at[half, y], at(k, 0))
            )
        for n, k in enumerate(reversed(x_order)):
            block = l_all.at[x, rows]
            sends.append(
                remote(block, block, ls_sem.at[half, n], lr_sem.at[half, x], at(0, k))
            )
        for copy in sends[start:]:
            copy.start()
        for n, r in enumerate(pair):
            for c in range(NX):
                for d in range(NY):
                    begin = n * 128 + c * 32 + d * 4
                    put(y32, (d * NX + c) * 16 + r, 4, wide[begin : begin + 4], stride=4)

    align_out[...] = jnp.concatenate([y32[0], y32[1]], axis=1).reshape(128, 4, 256).astype(BF16)

    def arrived(ref, peer, half, send_sem, recv_sem):
        block = ref.at[peer, pl.ds(half * 64, 64)]
        remote(block, block, send_sem.at[half, 0], recv_sem.at[half, peer], me).wait_recv()

    for half in range(2):
        for k in x_order:
            arrived(l_all, lax.rem(x + k, NX), half, ls_sem, lr_sem)
    left = l_all[...].reshape(NX * 128, 128)
    for half in range(2):
        for k in [0] + y_order:
            peer = lax.rem(y + k, NY)
            if k:
                arrived(r_all, peer, half, rs_sem, rr_sem)
            right = r_all[peer, half * 64 : (half + 1) * 64, :]
            product = dot_nt(right, left) * (1.0 / 128)
            for j in range(2):
                for e in range(0, 32, 8):
                    for n in range(NX):
                        start = e * 32 + (half * 2 + j) * 8 + peer
                        o32[n, pl.ds(start, 8, stride=32), :] = product[
                            j * 32 + e : j * 32 + e + 8, n * 128 : (n + 1) * 128
                        ]
    for e in range(32):
        ot[:, e * 128 : (e + 1) * 128] = jnp.concatenate(
            [o32[n, e * 32 : (e + 1) * 32, :] for n in range(NX)], axis=0
        ).astype(BF16)
    for half in range(2):
        product = dot(ot[...], bd[:, half * 256 : (half + 1) * 256])
        dsend[half] = product.astype(BF16).reshape(NX, 32, 256)
        for n, k in enumerate(reversed(x_order)):
            peer = lax.rem(x + k, NX)
            copy = remote(
                dsend.at[half, peer],
                drecv.at[half, x],
                ds_sem.at[half, n],
                dr_sem.at[half, x],
                at(0, k),
            )
            copy.start()
            sends.append(copy)
    drecv[:, x] = dsend[:, x]
    for k in [0] + x_order:
        peer = lax.rem(x + k, NX)
        for half in range(2):
            if k:
                block = drecv.at[half, peer]
                remote(
                    block, block, ds_sem.at[half, 0], dr_sem.at[half, peer], me
                ).wait_recv()
            block = drecv[half, peer].astype(F32)
            for i in range(2):
                for j in range(4):
                    f32s[pl.ds((half * 2 + i) * 128 + peer * 4 + j, 8, stride=16), :] = block[
                        j * 8 : (j + 1) * 8, i * 128 : (i + 1) * 128
                    ]
    pair_out[...] = (f32s[...] + two_v[...].reshape(512, 128).astype(F32)).astype(BF16).reshape(4, 128, 128)
    for copy in sends:
        copy.wait_send()


def per_device(hom, two, offset_map, win, wout, cwin, cwout, factors, tpe):
    operands = (hom, two, offset_map.T, win, wout, cwin, cwout, factors.T, tpe)
    operands = tuple(pltpu.with_memory_space_constraint(a, pltpu.HBM) for a in operands)
    dma = pltpu.SemaphoreType.DMA
    vm = pltpu.VMEM
    scratch = [vm(a.shape, BF16) for a in operands] + [
        vm((2, 512, 128), F32),
        vm((2, 512, 128), F32),
        vm((NX, 128, 256), BF16),
        vm((512, 256), BF16),
        vm((512, 256), BF16),
        vm((NX, 128, 256), F32),
        vm((NX, 128, 256), F32),
        vm((NX, 256, 128), F32),
        vm((ND, 32, 128), BF16),
        vm((NX, 2, 128, 128), F32),
        vm((ND, 16, 256), BF16),
        vm((ND, 16, 256), BF16),
        vm((2, 512, 128), F32),
        vm((NX, 128, 128), BF16),
        vm((NY, 128, 128), BF16),
        vm((NX, NY * 128, 128), F32),
        vm((128, 4096), BF16),
        vm((1024, 128), F32),
        vm((4096, 512), BF16),
        vm((2, NX, 32, 256), BF16),
        vm((2, NX, 32, 256), BF16),
        vm((512, 128), F32),
        dma((9,)),
        dma((31,)),
        dma((ND,)),
        dma,
        dma((NX,)),
        dma((2, 3)),
        dma((2, NX)),
        dma((2, 7)),
        dma((2, NY)),
        dma((2, 3)),
        dma((2, NX)),
    ]
    hbm = pl.BlockSpec(memory_space=pl.ANY)
    align, pair = pl.pallas_call(
        kernel,
        out_shape=(
            jax.ShapeDtypeStruct((128, 4, 256), BF16),
            jax.ShapeDtypeStruct((4, 128, 128), BF16),
        ),
        in_specs=[hbm] * len(operands),
        out_specs=(pl.BlockSpec(memory_space=pltpu.VMEM),) * 2,
        scratch_shapes=scratch,
        compiler_params=pltpu.CompilerParams(collective_id=0, has_side_effects=True, vmem_limit_bytes=40 * 2**20),
    )(*operands)
    return align, pair


def solution(mesh):
    split = P(("crop", "dap"), None, None)
    return jax.shard_map(
        per_device,
        mesh=mesh,
        in_specs=(split, split) + (P(),) * 7,
        out_specs=(P("crop", "dap", None), split),
        check_vma=False,
    )
```

```python
import math

import jax
import jax.numpy as jnp
from jax import lax
from jax.experimental import pallas as pl
from jax.experimental.pallas import tpu as pltpu
from jax.sharding import PartitionSpec as P

EPSILON = 1e-05
MESH = pl.DeviceIdType.MESH
F32 = jnp.float32
BF16 = jnp.bfloat16
LOG2E = math.log2(math.e)
NX = 4
NY = 8
ND = NX * NY
NT = (((1,), (1,)), ((), ()))


def standardized(values):
    center = values - jnp.mean(values, axis=-1, keepdims=True)
    spread = jnp.mean(center * center, axis=-1, keepdims=True)
    return center * lax.rsqrt(spread + EPSILON)


def dot(a, b):
    return jnp.dot(a, b, preferred_element_type=F32)


def dot_nt(a, b):
    return lax.dot_general(a, b, NT, preferred_element_type=F32)


def put(ref, start, size, value, stride=1):
    rows = pl.ds(start, size, stride=stride) if stride > 1 else pl.ds(start, size)
    for t in range(value.shape[1] // 128):
        ref[t, rows, :] = value[:, t * 128 : (t + 1) * 128]


def take(ref, start, size, stride):
    rows = pl.ds(start, size, stride=stride)
    return jnp.concatenate([ref[t, rows, :] for t in range(ref.shape[0])], axis=1)


def head_masks():
    lane = lax.broadcasted_iota(jnp.int32, (1, 128), 1)
    return [jnp.where(lane // 32 == h, 1.0, 0.0).astype(BF16) for h in range(4)]


def attend(q, k, v, gate, masks):
    scale = LOG2E / math.sqrt(32)
    weights = []
    values = []
    for h in range(4):
        scores = dot_nt(q * masks[h], k) * scale
        highest = jnp.max(scores, axis=-1, keepdims=True)
        weights.append(jnp.exp2(scores - highest).astype(BF16))
        ones = jnp.broadcast_to(masks[h], v.shape)
        values.append(jnp.concatenate([v * masks[h], ones], axis=1))
    both = dot(jnp.concatenate(weights, axis=1), jnp.concatenate(values, axis=0))
    return (jax.nn.sigmoid(gate) * (both[:, :128] / both[:, 128:])).astype(BF16)


def kernel(
    hom,
    two,
    map_t,
    win,
    wout,
    cwin,
    cwout,
    fac_t,
    tpe,
    align_out,
    pair_out,
    hom_v,
    two_v,
    map_v,
    win_v,
    wout_v,
    cwin_v,
    cwout_v,
    fac_v,
    tpe_v,
    x32,
    n32,
    q_s,
    k_s,
    v_s,
    g_s,
    xp,
    b32,
    bias_recv,
    m32,
    msend,
    mrecv,
    y32,
    l_all,
    r_all,
    o32,
    ot,
    w32,
    bd,
    dsend,
    drecv,
    f32s,
    in_sem,
    bs_sem,
    br_sem,
    ms_sem,
    mr_sem,
    ls_sem,
    lr_sem,
    rs_sem,
    rr_sem,
    ds_sem,
    dr_sem,
):
    me = lax.axis_index("dap")
    y = me // NX
    x = lax.rem(me, NX)

    def remote(src, dst, send_sem, recv_sem, target):
        return pltpu.make_async_remote_copy(
            src_ref=src,
            dst_ref=dst,
            send_sem=send_sem,
            recv_sem=recv_sem,
            device_id={"dap": target},
            device_id_type=MESH,
        )

    pairs = [
        (two, two_v),
        (map_t, map_v),
        (hom, hom_v),
        (win, win_v),
        (tpe, tpe_v),
        (wout, wout_v),
        (cwin, cwin_v),
        (cwout, cwout_v),
        (fac_t, fac_v),
    ]
    loads = [pltpu.make_async_copy(a, b, in_sem.at[n]) for n, (a, b) in enumerate(pairs)]
    for load in loads:
        load.start()
    names = ("two", "map", "hom", "win", "tpe", "wout", "cwin", "cwout", "fac")
    ready = dict(zip(names, loads))

    barrier = pltpu.get_barrier_semaphore()

    y_order = [1, 7, 2, 6, 3, 5, 4]
    x_order = [1, 3, 2]

    def at(dy, dx):
        return lax.rem(y + dy, NY) * NX + lax.rem(x + dx, NX)

    for dy, dx in [(k, 0) for k in reversed(y_order)] + [(0, k) for k in reversed(x_order)]:
        pl.semaphore_signal(barrier, inc=1, device_id={"dap": at(dy, dx)}, device_id_type=MESH)

    ready["two"].wait()
    ready["map"].wait()
    for i in range(4):
        pair_norm = standardized(two_v[i].astype(F32)).astype(BF16)
        b32[0, pl.ds(i, 8, stride=4), :] = dot_nt(map_v[...], pair_norm)
    bias_recv[me] = b32[0, 0:32, :].astype(BF16)

    pl.semaphore_wait(barrier, NY + NX - 2)

    bias_sends = []

    def send_bias(block, target):
        copy = remote(
            bias_recv.at[block],
            bias_recv.at[block],
            bs_sem.at[len(bias_sends)],
            br_sem.at[block],
            target,
        )
        copy.start()
        bias_sends.append(copy)

    def bias_arrived(block):
        remote(
            bias_recv.at[block], bias_recv.at[block], bs_sem.at[0], br_sem.at[block], me
        ).wait_recv()

    for k in reversed(y_order):
        send_bias(me, at(k, 0))
    for k in (1, 3):
        send_bias(me, at(0, k))

    ready["hom"].wait()
    ready["win"].wait()
    masks = head_masks()
    wide_masks = [jnp.concatenate([mask, mask], axis=1).astype(F32) for mask in masks]
    values = hom_v[...].reshape(512, 256).astype(F32)
    put(x32, 0, 512, values)
    normal = standardized(values)
    put(n32, 0, 512, normal)
    normal = normal.astype(BF16)
    k_s[...] = dot(normal, win_v[:, 256:512]).astype(BF16)
    v_s[...] = dot(normal, win_v[:, 512:768]).astype(BF16)

    def mixed(ref, group):
        return jnp.concatenate(
            [take(ref, s * 128 + group * 4 + i, 8, 16) for s in range(4) for i in range(4)],
            axis=0,
        )

    normal = jnp.concatenate([mixed(n32, group) for group in range(NX)], axis=0).astype(BF16)
    q_s[...] = dot(normal, win_v[:, 0:256]).astype(BF16).reshape(NX, 128, 256)
    gates = dot(normal, win_v[:, 768:1024]).astype(BF16).astype(F32)
    g_s[...] = jax.nn.sigmoid(gates).reshape(NX, 128, 256)
    for group in range(NX):
        xp[group] = mixed(x32, group)

    ready["tpe"].wait()
    w32[...] = tpe_v[...].astype(F32)
    bd[...] = jnp.zeros_like(bd)
    for e in range(32):
        piece = w32[pl.ds(e, 32, stride=32), :].astype(BF16)
        for i in range(4):
            bd[e * 128 + i * 32 : e * 128 + (i + 1) * 32, i * 128 : (i + 1) * 128] = piece

    for k in y_order:
        block = at(k, 0)
        bias_arrived(block)
        for m in (1, 3):
            send_bias(block, at(0, m))

    ready["wout"].wait()
    scale = LOG2E / math.sqrt(32)
    ones = jnp.ones((128, 128), BF16)
    for n, m in enumerate([0, 1, 3, 2]):
        column = lax.rem(x + m, NX)
        if m == 1:
            for k in [0] + y_order:
                for dx in (1, 3):
                    bias_arrived(at(k, dx))
                send_bias(at(k, 1 if k % 2 else 3), at(0, 3 if k % 2 else 1))
        if m == 2:
            for k in [0] + y_order:
                bias_arrived(at(k, m))
        for r in range(NY):
            b32[n, r * 32 : (r + 1) * 32, :] = bias_recv[r * NX + column].astype(F32) * LOG2E
        bias = [
            jnp.concatenate(
                [b32[n, pl.ds(g * 16 + i, 8, stride=32), :] for i in range(16)], axis=0
            )
            for g in range(2)
        ]
        parts = []
        for g in range(2):
            lanes = slice(g * 128, (g + 1) * 128)
            part = []
            for s in range(4):
                rows = slice(s * 32, (s + 1) * 32)
                query = q_s[column, rows, lanes]
                query = jnp.concatenate([query * mask for mask in masks], axis=0)
                scores = dot_nt(query, k_s[s * 128 : (s + 1) * 128, lanes]) * scale + bias[g]
                highest = jnp.max(scores, axis=-1, keepdims=True)
                weights = jnp.exp2(scores - highest).astype(BF16)
                value = jnp.concatenate([v_s[s * 128 : (s + 1) * 128, lanes], ones], axis=1)
                both = dot(weights, value)
                both = sum(
                    both[h * 32 : (h + 1) * 32] * wide_masks[h] for h in range(4)
                )
                part.append(both[:, :128] / both[:, 128:] * g_s[column, rows, lanes])
            parts.append(jnp.concatenate(part, axis=0).astype(BF16))
        total = xp[column] + dot(jnp.concatenate(parts, axis=1), wout_v[...])
        for s in range(4):
            for i in range(4):
                start = s * 32 + i * 8
                for t in range(2):
                    m32[n, t, pl.ds(i * 4 + s, 8, stride=16), :] = total[
                        start : start + 8, t * 128 : (t + 1) * 128
                    ]
        for r in range(NY):
            rows = slice(r * 16, (r + 1) * 16)
            msend[r * NX + column] = jnp.concatenate(
                [m32[n, 0, rows, :], m32[n, 1, rows, :]], axis=1
            ).astype(BF16)
        if not m:
            mrecv[me] = msend[me]
        for k in list(reversed(y_order)) + ([] if m == 0 else [0]):
            target = at(k, m)
            remote(msend.at[target], mrecv.at[me], ms_sem, mr_sem.at[m], target).start()

    for copy in bias_sends:
        copy.wait_send()
    for name in ("cwin", "cwout", "fac"):
        ready[name].wait()

    for m in range(NX):
        column = lax.rem(x + NX - m, NX)
        count = NY - 1 if m == 0 else NY
        group = mrecv.at[pl.ds(0, count)]
        remote(group, group, ms_sem, mr_sem.at[m], me).wait_recv()
        values = jnp.concatenate([mrecv[r * NX + column] for r in range(NY)], axis=0).astype(F32)
        normal = standardized(values)
        base = pl.multiple_of(column * 32, 32)
        for r in range(NY):
            for i in range(4):
                start = r * 16 + i * 4
                for t in range(2):
                    lanes = slice(t * 128, (t + 1) * 128)
                    x32.at[t, pl.ds(i * 128 + base, 32), :][r * 4 : (r + 1) * 4, :] = values[
                        start : start + 4, lanes
                    ]
                    n32.at[t, pl.ds(i * 128 + base, 32), :][r * 4 : (r + 1) * 4, :] = normal[
                        start : start + 4, lanes
                    ]
    everything = msend.at[pl.ds(0, ND - 1)]
    remote(everything, everything, ms_sem, mr_sem.at[0], me).wait_send()

    def arrived(ref, peer, half, send_sem, recv_sem):
        block = ref.at[peer, pl.ds(half * 64, 64)]
        remote(block, block, send_sem.at[half, 0], recv_sem.at[half, peer], me).wait_recv()

    sends = []

    def pass_on(half):
        slot = 4
        for k in (2, 6):
            peer = lax.rem(y + k, NY)
            arrived(r_all, peer, half, rs_sem, rr_sem)
            block = r_all.at[peer, pl.ds(half * 64, 64)]
            targets = [1 if k == 6 else 7]
            if (k == 6) == (half == 0):
                targets = [2 if k == 6 else 6] + targets
            for target in targets:
                copy = remote(
                    block, block, rs_sem.at[half, slot], rr_sem.at[half, peer], at(target, 0)
                )
                copy.start()
                sends.append(copy)
                slot += 1

    for half in range(2):
        pair = (half * 2, half * 2 + 1)
        rows = slice(half * 256, (half + 1) * 256)
        values = jnp.concatenate([x32[0, rows, :], x32[1, rows, :]], axis=1)
        normal = jnp.concatenate([n32[0, rows, :], n32[1, rows, :]], axis=1).astype(BF16)
        packed = [dot(normal, cwin_v[:, n * 256 : (n + 1) * 256]).astype(BF16) for n in range(4)]
        gated = []
        for n in range(2):
            parts = []
            for g in range(2):
                q, k, v, gate = [
                    part[n * 128 : (n + 1) * 128, g * 128 : (g + 1) * 128] for part in packed
                ]
                parts.append(attend(q, k, v, gate.astype(F32), masks))
            gated.append(jnp.concatenate(parts, axis=1))
        total = values + dot(jnp.concatenate(gated, axis=0), cwout_v[...])
        wide = total.astype(BF16).astype(F32)
        factors = dot_nt(fac_v[...], standardized(wide).astype(BF16)).astype(BF16)
        for n, r in enumerate(pair):
            l_all[x, r * 32 : (r + 1) * 32, :] = factors[:32, n * 128 : (n + 1) * 128]
            r_all[y, r * 32 : (r + 1) * 32, :] = factors[32:, n * 128 : (n + 1) * 128]
        rows = pl.ds(half * 64, 64)
        start = len(sends)
        for n, k in enumerate((2, 6, 1, 7)):
            block = r_all.at[y, rows]
            sends.append(
                remote(block, block, rs_sem.at[half, n], rr_sem.at[half, y], at(k, 0))
            )
        for n, k in enumerate(reversed(x_order)):
            block = l_all.at[x, rows]
            sends.append(
                remote(block, block, ls_sem.at[half, n], lr_sem.at[half, x], at(0, k))
            )
        for copy in sends[start:]:
            copy.start()
        if half:
            pass_on(0)
        for n, r in enumerate(pair):
            for c in range(NX):
                for d in range(NY):
                    begin = n * 128 + c * 32 + d * 4
                    put(y32, (d * NX + c) * 16 + r, 4, wide[begin : begin + 4], stride=4)

    align_out[...] = jnp.concatenate([y32[0], y32[1]], axis=1).reshape(128, 4, 256).astype(BF16)

    pass_on(1)
    for half in range(2):
        for k in x_order:
            arrived(l_all, lax.rem(x + k, NX), half, ls_sem, lr_sem)
    left = l_all[...].reshape(NX * 128, 128)
    for half in range(2):
        for k in [0] + y_order:
            peer = lax.rem(y + k, NY)
            if k not in (0, 2, 6):
                arrived(r_all, peer, half, rs_sem, rr_sem)
            right = r_all[peer, half * 64 : (half + 1) * 64, :]
            product = dot_nt(right, left) * (1.0 / 128)
            for j in range(2):
                for e in range(0, 32, 8):
                    for n in range(NX):
                        start = e * 32 + (half * 2 + j) * 8 + peer
                        o32[n, pl.ds(start, 8, stride=32), :] = product[
                            j * 32 + e : j * 32 + e + 8, n * 128 : (n + 1) * 128
                        ]
    for e in range(32):
        ot[:, e * 128 : (e + 1) * 128] = jnp.concatenate(
            [o32[n, e * 32 : (e + 1) * 32, :] for n in range(NX)], axis=0
        ).astype(BF16)
    for half in range(2):
        product = dot(ot[...], bd[:, half * 256 : (half + 1) * 256])
        dsend[half] = product.astype(BF16).reshape(NX, 32, 256)
        for n, k in enumerate(reversed(x_order)):
            peer = lax.rem(x + k, NX)
            copy = remote(
                dsend.at[half, peer],
                drecv.at[half, x],
                ds_sem.at[half, n],
                dr_sem.at[half, x],
                at(0, k),
            )
            copy.start()
            sends.append(copy)
    drecv[:, x] = dsend[:, x]
    for k in [0] + x_order:
        peer = lax.rem(x + k, NX)
        for half in range(2):
            if k:
                block = drecv.at[half, peer]
                remote(
                    block, block, ds_sem.at[half, 0], dr_sem.at[half, peer], me
                ).wait_recv()
            block = drecv[half, peer].astype(F32)
            for i in range(2):
                for j in range(4):
                    f32s[pl.ds((half * 2 + i) * 128 + peer * 4 + j, 8, stride=16), :] = block[
                        j * 8 : (j + 1) * 8, i * 128 : (i + 1) * 128
                    ]
    pair_out[...] = (f32s[...] + two_v[...].reshape(512, 128).astype(F32)).astype(BF16).reshape(4, 128, 128)
    for copy in sends:
        copy.wait_send()


def per_device(hom, two, offset_map, win, wout, cwin, cwout, factors, tpe):
    operands = (hom, two, offset_map.T, win, wout, cwin, cwout, factors.T, tpe)
    operands = tuple(pltpu.with_memory_space_constraint(a, pltpu.HBM) for a in operands)
    dma = pltpu.SemaphoreType.DMA
    vm = pltpu.VMEM
    scratch = [vm(a.shape, BF16) for a in operands] + [
        vm((2, 512, 128), F32),
        vm((2, 512, 128), F32),
        vm((NX, 128, 256), BF16),
        vm((512, 256), BF16),
        vm((512, 256), BF16),
        vm((NX, 128, 256), F32),
        vm((NX, 128, 256), F32),
        vm((NX, 256, 128), F32),
        vm((ND, 32, 128), BF16),
        vm((NX, 2, 128, 128), F32),
        vm((ND, 16, 256), BF16),
        vm((ND, 16, 256), BF16),
        vm((2, 512, 128), F32),
        vm((NX, 128, 128), BF16),
        vm((NY, 128, 128), BF16),
        vm((NX, NY * 128, 128), F32),
        vm((128, 4096), BF16),
        vm((1024, 128), F32),
        vm((4096, 512), BF16),
        vm((2, NX, 32, 256), BF16),
        vm((2, NX, 32, 256), BF16),
        vm((512, 128), F32),
        dma((9,)),
        dma((31,)),
        dma((ND,)),
        dma,
        dma((NX,)),
        dma((2, 3)),
        dma((2, NX)),
        dma((2, 7)),
        dma((2, NY)),
        dma((2, 3)),
        dma((2, NX)),
    ]
    hbm = pl.BlockSpec(memory_space=pl.ANY)
    align, pair = pl.pallas_call(
        kernel,
        out_shape=(
            jax.ShapeDtypeStruct((128, 4, 256), BF16),
            jax.ShapeDtypeStruct((4, 128, 128), BF16),
        ),
        in_specs=[hbm] * len(operands),
        out_specs=(pl.BlockSpec(memory_space=pltpu.VMEM),) * 2,
        scratch_shapes=scratch,
        compiler_params=pltpu.CompilerParams(collective_id=0, has_side_effects=True, vmem_limit_bytes=40 * 2**20),
    )(*operands)
    return align, pair


def solution(mesh):
    split = P(("crop", "dap"), None, None)
    return jax.shard_map(
        per_device,
        mesh=mesh,
        in_specs=(split, split) + (P(),) * 7,
        out_specs=(P("crop", "dap", None), split),
        check_vma=False,
    )
```

```python
import math

import jax
import jax.numpy as jnp
from jax import lax
from jax.experimental import pallas as pl
from jax.experimental.pallas import tpu as pltpu
from jax.sharding import PartitionSpec as P

EPSILON = 1e-05
MESH = pl.DeviceIdType.MESH
F32 = jnp.float32
BF16 = jnp.bfloat16
LOG2E = math.log2(math.e)
NX = 4
NY = 8
ND = NX * NY
NT = (((1,), (1,)), ((), ()))


def standardized(values):
    center = values - jnp.mean(values, axis=-1, keepdims=True)
    spread = jnp.mean(center * center, axis=-1, keepdims=True)
    return center * lax.rsqrt(spread + EPSILON)


def dot(a, b):
    return jnp.dot(a, b, preferred_element_type=F32)


def dot_nt(a, b):
    return lax.dot_general(a, b, NT, preferred_element_type=F32)


def put(ref, start, size, value, stride=1):
    rows = pl.ds(start, size, stride=stride) if stride > 1 else pl.ds(start, size)
    for t in range(value.shape[1] // 128):
        ref[t, rows, :] = value[:, t * 128 : (t + 1) * 128]


def take(ref, start, size, stride):
    rows = pl.ds(start, size, stride=stride)
    return jnp.concatenate([ref[t, rows, :] for t in range(ref.shape[0])], axis=1)


def head_masks():
    lane = lax.broadcasted_iota(jnp.int32, (1, 128), 1)
    return [jnp.where(lane // 32 == h, 1.0, 0.0).astype(BF16) for h in range(4)]


def attend(q, k, v, gate, masks):
    scale = LOG2E / math.sqrt(32)
    weights = []
    values = []
    for h in range(4):
        scores = dot_nt(q * masks[h], k) * scale
        highest = jnp.max(scores, axis=-1, keepdims=True)
        weights.append(jnp.exp2(scores - highest).astype(BF16))
        ones = jnp.broadcast_to(masks[h], v.shape)
        values.append(jnp.concatenate([v * masks[h], ones], axis=1))
    both = dot(jnp.concatenate(weights, axis=1), jnp.concatenate(values, axis=0))
    return (jax.nn.sigmoid(gate) * (both[:, :128] / both[:, 128:])).astype(BF16)


def kernel(
    hom,
    two,
    map_t,
    win,
    wout,
    cwin,
    cwout,
    fac_t,
    tpe,
    align_out,
    pair_out,
    hom_v,
    two_v,
    map_v,
    win_v,
    wout_v,
    cwin_v,
    cwout_v,
    fac_v,
    tpe_v,
    x32,
    n32,
    q_s,
    k_s,
    v_s,
    g_s,
    xp,
    b32,
    bias_recv,
    m32,
    msend,
    mrecv,
    y32,
    l_all,
    r_all,
    o32,
    ot,
    w32,
    bd,
    dsend,
    drecv,
    f32s,
    in_sem,
    bs_sem,
    br_sem,
    ms_sem,
    mr_sem,
    ls_sem,
    lr_sem,
    rs_sem,
    rr_sem,
    ds_sem,
    dr_sem,
):
    me = lax.axis_index("dap")
    y = me // NX
    x = lax.rem(me, NX)

    def remote(src, dst, send_sem, recv_sem, target):
        return pltpu.make_async_remote_copy(
            src_ref=src,
            dst_ref=dst,
            send_sem=send_sem,
            recv_sem=recv_sem,
            device_id={"dap": target},
            device_id_type=MESH,
        )

    pairs = [
        (two, two_v),
        (map_t, map_v),
        (hom, hom_v),
        (win, win_v),
        (tpe, tpe_v),
        (wout, wout_v),
        (cwin, cwin_v),
        (cwout, cwout_v),
        (fac_t, fac_v),
    ]
    loads = [pltpu.make_async_copy(a, b, in_sem.at[n]) for n, (a, b) in enumerate(pairs)]
    for load in loads:
        load.start()
    names = ("two", "map", "hom", "win", "tpe", "wout", "cwin", "cwout", "fac")
    ready = dict(zip(names, loads))

    barrier = pltpu.get_barrier_semaphore()

    y_order = [1, 7, 2, 6, 3, 5, 4]
    x_order = [1, 3, 2]

    def at(dy, dx):
        return lax.rem(y + dy, NY) * NX + lax.rem(x + dx, NX)

    for dy, dx in [(k, 0) for k in reversed(y_order)] + [(0, k) for k in reversed(x_order)]:
        pl.semaphore_signal(barrier, inc=1, device_id={"dap": at(dy, dx)}, device_id_type=MESH)

    ready["two"].wait()
    ready["map"].wait()
    for i in range(4):
        pair_norm = standardized(two_v[i].astype(F32)).astype(BF16)
        b32[0, pl.ds(i, 8, stride=4), :] = dot_nt(map_v[...], pair_norm)
    bias_recv[me] = b32[0, 0:32, :].astype(BF16)

    pl.semaphore_wait(barrier, NY + NX - 2)

    bias_sends = []

    def send_bias(block, target):
        copy = remote(
            bias_recv.at[block],
            bias_recv.at[block],
            bs_sem.at[len(bias_sends)],
            br_sem.at[block],
            target,
        )
        copy.start()
        bias_sends.append(copy)

    def bias_arrived(block):
        remote(
            bias_recv.at[block], bias_recv.at[block], bs_sem.at[0], br_sem.at[block], me
        ).wait_recv()

    for k in reversed(y_order):
        send_bias(me, at(k, 0))
    for k in reversed(x_order):
        send_bias(me, at(0, k))

    ready["hom"].wait()
    ready["win"].wait()
    masks = head_masks()
    wide_masks = [jnp.concatenate([mask, mask], axis=1).astype(F32) for mask in masks]
    values = hom_v[...].reshape(512, 256).astype(F32)
    put(x32, 0, 512, values)
    normal = standardized(values)
    put(n32, 0, 512, normal)
    normal = normal.astype(BF16)
    k_s[...] = dot(normal, win_v[:, 256:512]).astype(BF16)
    v_s[...] = dot(normal, win_v[:, 512:768]).astype(BF16)

    def mixed(ref, group):
        return jnp.concatenate(
            [take(ref, s * 128 + group * 4 + i, 8, 16) for s in range(4) for i in range(4)],
            axis=0,
        )

    normal = jnp.concatenate([mixed(n32, group) for group in range(NX)], axis=0).astype(BF16)
    q_s[...] = dot(normal, win_v[:, 0:256]).astype(BF16).reshape(NX, 128, 256)
    gates = dot(normal, win_v[:, 768:1024]).astype(BF16).astype(F32)
    g_s[...] = jax.nn.sigmoid(gates).reshape(NX, 128, 256)
    for group in range(NX):
        xp[group] = mixed(x32, group)

    ready["tpe"].wait()
    w32[...] = tpe_v[...].astype(F32)
    bd[...] = jnp.zeros_like(bd)
    for e in range(32):
        piece = w32[pl.ds(e, 32, stride=32), :].astype(BF16)
        for i in range(4):
            bd[e * 128 + i * 32 : e * 128 + (i + 1) * 32, i * 128 : (i + 1) * 128] = piece

    for k in y_order:
        block = at(k, 0)
        bias_arrived(block)
        for m in reversed(x_order):
            send_bias(block, at(0, m))

    ready["wout"].wait()
    scale = LOG2E / math.sqrt(32)
    ones = jnp.ones((128, 128), BF16)
    for n, m in enumerate([0, 1, 2, 3]):
        column = lax.rem(x + m, NX)
        if m:
            for k in [0] + y_order:
                bias_arrived(at(k, m))
        for r in range(NY):
            b32[n, r * 32 : (r + 1) * 32, :] = bias_recv[r * NX + column].astype(F32) * LOG2E
        bias = [
            jnp.concatenate(
                [b32[n, pl.ds(g * 16 + i, 8, stride=32), :] for i in range(16)], axis=0
            )
            for g in range(2)
        ]
        parts = []
        for g in range(2):
            lanes = slice(g * 128, (g + 1) * 128)
            part = []
            for s in range(4):
                rows = slice(s * 32, (s + 1) * 32)
                query = q_s[column, rows, lanes]
                query = jnp.concatenate([query * mask for mask in masks], axis=0)
                scores = dot_nt(query, k_s[s * 128 : (s + 1) * 128, lanes]) * scale + bias[g]
                highest = jnp.max(scores, axis=-1, keepdims=True)
                weights = jnp.exp2(scores - highest).astype(BF16)
                value = jnp.concatenate([v_s[s * 128 : (s + 1) * 128, lanes], ones], axis=1)
                both = dot(weights, value)
                both = sum(
                    both[h * 32 : (h + 1) * 32] * wide_masks[h] for h in range(4)
                )
                part.append(both[:, :128] / both[:, 128:] * g_s[column, rows, lanes])
            parts.append(jnp.concatenate(part, axis=0).astype(BF16))
        total = xp[column] + dot(jnp.concatenate(parts, axis=1), wout_v[...])
        for s in range(4):
            for i in range(4):
                start = s * 32 + i * 8
                for t in range(2):
                    m32[n, t, pl.ds(i * 4 + s, 8, stride=16), :] = total[
                        start : start + 8, t * 128 : (t + 1) * 128
                    ]
        for r in range(NY):
            rows = slice(r * 16, (r + 1) * 16)
            msend[r * NX + column] = jnp.concatenate(
                [m32[n, 0, rows, :], m32[n, 1, rows, :]], axis=1
            ).astype(BF16)
        if not m:
            mrecv[me] = msend[me]
        for k in list(reversed(y_order)) + ([] if m == 0 else [0]):
            target = at(k, m)
            remote(msend.at[target], mrecv.at[me], ms_sem, mr_sem.at[m], target).start()

    for copy in bias_sends:
        copy.wait_send()
    for name in ("cwin", "cwout", "fac"):
        ready[name].wait()

    for m in range(NX):
        column = lax.rem(x + NX - m, NX)
        count = NY - 1 if m == 0 else NY
        group = mrecv.at[pl.ds(0, count)]
        remote(group, group, ms_sem, mr_sem.at[m], me).wait_recv()
        values = jnp.concatenate([mrecv[r * NX + column] for r in range(NY)], axis=0).astype(F32)
        normal = standardized(values)
        base = pl.multiple_of(column * 32, 32)
        for r in range(NY):
            for i in range(4):
                start = r * 16 + i * 4
                for t in range(2):
                    lanes = slice(t * 128, (t + 1) * 128)
                    x32.at[t, pl.ds(i * 128 + base, 32), :][r * 4 : (r + 1) * 4, :] = values[
                        start : start + 4, lanes
                    ]
                    n32.at[t, pl.ds(i * 128 + base, 32), :][r * 4 : (r + 1) * 4, :] = normal[
                        start : start + 4, lanes
                    ]
    everything = msend.at[pl.ds(0, ND - 1)]
    remote(everything, everything, ms_sem, mr_sem.at[0], me).wait_send()

    sends = []
    for half in range(2):
        pair = (half * 2, half * 2 + 1)
        rows = slice(half * 256, (half + 1) * 256)
        values = jnp.concatenate([x32[0, rows, :], x32[1, rows, :]], axis=1)
        normal = jnp.concatenate([n32[0, rows, :], n32[1, rows, :]], axis=1).astype(BF16)
        packed = [dot(normal, cwin_v[:, n * 256 : (n + 1) * 256]).astype(BF16) for n in range(4)]
        gated = []
        for n in range(2):
            parts = []
            for g in range(2):
                q, k, v, gate = [
                    part[n * 128 : (n + 1) * 128, g * 128 : (g + 1) * 128] for part in packed
                ]
                parts.append(attend(q, k, v, gate.astype(F32), masks))
            gated.append(jnp.concatenate(parts, axis=1))
        total = values + dot(jnp.concatenate(gated, axis=0), cwout_v[...])
        wide = total.astype(BF16).astype(F32)
        factors = dot_nt(fac_v[...], standardized(wide).astype(BF16)).astype(BF16)
        for n, r in enumerate(pair):
            l_all[x, r * 32 : (r + 1) * 32, :] = factors[:32, n * 128 : (n + 1) * 128]
            r_all[y, r * 32 : (r + 1) * 32, :] = factors[32:, n * 128 : (n + 1) * 128]
        rows = pl.ds(half * 64, 64)
        start = len(sends)
        for n, k in enumerate(reversed(y_order)):
            block = r_all.at[y, rows]
            sends.append(
                remote(block, block, rs_sem.at[half, n], rr_sem.at[half, y], at(k, 0))
            )
        for n, k in enumerate(reversed(x_order)):
            block = l_all.at[x, rows]
            sends.append(
                remote(block, block, ls_sem.at[half, n], lr_sem.at[half, x], at(0, k))
            )
        for copy in sends[start:]:
            copy.start()
        for n, r in enumerate(pair):
            for c in range(NX):
                for d in range(NY):
                    begin = n * 128 + c * 32 + d * 4
                    put(y32, (d * NX + c) * 16 + r, 4, wide[begin : begin + 4], stride=4)

    align_out[...] = jnp.concatenate([y32[0], y32[1]], axis=1).reshape(128, 4, 256).astype(BF16)

    def arrived(ref, peer, half, send_sem, recv_sem):
        block = ref.at[peer, pl.ds(half * 64, 64)]
        remote(block, block, send_sem.at[half, 0], recv_sem.at[half, peer], me).wait_recv()

    for half in range(2):
        for k in x_order:
            arrived(l_all, lax.rem(x + k, NX), half, ls_sem, lr_sem)
    left = l_all[...].reshape(NX * 128, 128)
    for half in range(2):
        for k in [0] + y_order:
            peer = lax.rem(y + k, NY)
            if k:
                arrived(r_all, peer, half, rs_sem, rr_sem)
            right = r_all[peer, half * 64 : (half + 1) * 64, :]
            product = dot_nt(right, left) * (1.0 / 128)
            for j in range(2):
                for e in range(0, 32, 8):
                    for n in range(NX):
                        start = e * 32 + (half * 2 + j) * 8 + peer
                        o32[n, pl.ds(start, 8, stride=32), :] = product[
                            j * 32 + e : j * 32 + e + 8, n * 128 : (n + 1) * 128
                        ]
    for e in range(32):
        ot[:, e * 128 : (e + 1) * 128] = jnp.concatenate(
            [o32[n, e * 32 : (e + 1) * 32, :] for n in range(NX)], axis=0
        ).astype(BF16)
    dsend[...] = dot(ot[...], bd[...]).astype(BF16).reshape(NX, 32, 512)
    for n, k in enumerate(reversed(x_order)):
        peer = lax.rem(x + k, NX)
        copy = remote(dsend.at[peer], drecv.at[x], ds_sem.at[n], dr_sem.at[x], at(0, k))
        copy.start()
        sends.append(copy)
    drecv[x] = dsend[x]
    for k in [0] + x_order:
        peer = lax.rem(x + k, NX)
        if k:
            block = drecv.at[peer]
            remote(block, block, ds_sem.at[0], dr_sem.at[peer], me).wait_recv()
        block = drecv[peer].astype(F32)
        for i in range(4):
            for j in range(4):
                f32s[pl.ds(i * 128 + peer * 4 + j, 8, stride=16), :] = block[
                    j * 8 : (j + 1) * 8, i * 128 : (i + 1) * 128
                ]
    pair_out[...] = (f32s[...] + two_v[...].reshape(512, 128).astype(F32)).astype(BF16).reshape(4, 128, 128)
    for copy in sends:
        copy.wait_send()


def write_out(align, pair, align_out, pair_out, sem):
    copies = [
        pltpu.make_async_copy(align, align_out, sem.at[0]),
        pltpu.make_async_copy(pair, pair_out, sem.at[1]),
    ]
    for copy in copies:
        copy.start()
    for copy in copies:
        copy.wait()


def per_device(hom, two, offset_map, win, wout, cwin, cwout, factors, tpe):
    operands = (hom, two, offset_map.T, win, wout, cwin, cwout, factors.T, tpe)
    operands = tuple(pltpu.with_memory_space_constraint(a, pltpu.HBM) for a in operands)
    dma = pltpu.SemaphoreType.DMA
    vm = pltpu.VMEM
    scratch = [vm(a.shape, BF16) for a in operands] + [
        vm((2, 512, 128), F32),
        vm((2, 512, 128), F32),
        vm((NX, 128, 256), BF16),
        vm((512, 256), BF16),
        vm((512, 256), BF16),
        vm((NX, 128, 256), F32),
        vm((NX, 128, 256), F32),
        vm((NX, 256, 128), F32),
        vm((ND, 32, 128), BF16),
        vm((NX, 2, 128, 128), F32),
        vm((ND, 16, 256), BF16),
        vm((ND, 16, 256), BF16),
        vm((2, 512, 128), F32),
        vm((NX, 128, 128), BF16),
        vm((NY, 128, 128), BF16),
        vm((NX, NY * 128, 128), F32),
        vm((128, 4096), BF16),
        vm((1024, 128), F32),
        vm((4096, 512), BF16),
        vm((NX, 32, 512), BF16),
        vm((NX, 32, 512), BF16),
        vm((512, 128), F32),
        dma((9,)),
        dma((31,)),
        dma((ND,)),
        dma,
        dma((NX,)),
        dma((2, 3)),
        dma((2, NX)),
        dma((2, 7)),
        dma((2, NY)),
        dma((3,)),
        dma((NX,)),
    ]
    hbm = pl.BlockSpec(memory_space=pl.ANY)
    align, pair = pl.pallas_call(
        kernel,
        out_shape=(
            jax.ShapeDtypeStruct((128, 4, 256), BF16),
            jax.ShapeDtypeStruct((4, 128, 128), BF16),
        ),
        in_specs=[hbm] * len(operands),
        out_specs=(pl.BlockSpec(memory_space=pltpu.VMEM),) * 2,
        scratch_shapes=scratch,
        compiler_params=pltpu.CompilerParams(collective_id=0, has_side_effects=True, vmem_limit_bytes=40 * 2**20),
    )(*operands)
    return pl.pallas_call(
        write_out,
        out_shape=(
            jax.ShapeDtypeStruct((128, 4, 256), BF16),
            jax.ShapeDtypeStruct((4, 128, 128), BF16),
        ),
        in_specs=[pl.BlockSpec(memory_space=pltpu.VMEM)] * 2,
        out_specs=(hbm, hbm),
        scratch_shapes=[dma((2,))],
        compiler_params=pltpu.CompilerParams(vmem_limit_bytes=40 * 2**20),
    )(align, pair)


def solution(mesh):
    split = P(("crop", "dap"), None, None)
    return jax.shard_map(
        per_device,
        mesh=mesh,
        in_specs=(split, split) + (P(),) * 7,
        out_specs=(P("crop", "dap", None), split),
        check_vma=False,
    )
```

```python
import math

import jax
import jax.numpy as jnp
from jax import lax
from jax.experimental import pallas as pl
from jax.experimental.pallas import tpu as pltpu
from jax.sharding import PartitionSpec as P

EPSILON = 1e-05
MESH = pl.DeviceIdType.MESH
F32 = jnp.float32
BF16 = jnp.bfloat16
LOG2E = math.log2(math.e)
NX = 4
NY = 8
ND = NX * NY
NT = (((1,), (1,)), ((), ()))


def standardized(values):
    center = values - jnp.mean(values, axis=-1, keepdims=True)
    spread = jnp.mean(center * center, axis=-1, keepdims=True)
    return center * lax.rsqrt(spread + EPSILON)


def dot(a, b):
    return jnp.dot(a, b, preferred_element_type=F32)


def dot_nt(a, b):
    return lax.dot_general(a, b, NT, preferred_element_type=F32)


def put(ref, start, size, value, stride=1):
    rows = pl.ds(start, size, stride=stride) if stride > 1 else pl.ds(start, size)
    for t in range(value.shape[1] // 128):
        ref[t, rows, :] = value[:, t * 128 : (t + 1) * 128]


def take(ref, start, size, stride):
    rows = pl.ds(start, size, stride=stride)
    return jnp.concatenate([ref[t, rows, :] for t in range(ref.shape[0])], axis=1)


def head_masks():
    lane = lax.broadcasted_iota(jnp.int32, (1, 128), 1)
    return [jnp.where(lane // 32 == h, 1.0, 0.0).astype(BF16) for h in range(4)]


def attend(q, k, v, gate, masks):
    scale = LOG2E / math.sqrt(32)
    weights = []
    values = []
    for h in range(4):
        scores = dot_nt(q * masks[h], k) * scale
        highest = jnp.max(scores, axis=-1, keepdims=True)
        weights.append(jnp.exp2(scores - highest).astype(BF16))
        ones = jnp.broadcast_to(masks[h], v.shape)
        values.append(jnp.concatenate([v * masks[h], ones], axis=1))
    both = dot(jnp.concatenate(weights, axis=1), jnp.concatenate(values, axis=0))
    return (jax.nn.sigmoid(gate) * (both[:, :128] / both[:, 128:])).astype(BF16)


def kernel(
    hom,
    two,
    map_t,
    win,
    wout,
    cwin,
    cwout,
    fac_t,
    tpe,
    align_out,
    pair_out,
    hom_v,
    two_v,
    map_v,
    win_v,
    wout_v,
    cwin_v,
    cwout_v,
    fac_v,
    tpe_v,
    x32,
    n32,
    q_s,
    k_s,
    v_s,
    g_s,
    sc,
    xp,
    b32,
    bias_recv,
    m32,
    msend,
    mrecv,
    y32,
    l_all,
    r_all,
    o32,
    ot,
    w32,
    bd,
    dsend,
    drecv,
    f32s,
    in_sem,
    bs_sem,
    br_sem,
    ms_sem,
    mr_sem,
    ls_sem,
    lr_sem,
    rs_sem,
    rr_sem,
    ds_sem,
    dr_sem,
):
    me = lax.axis_index("dap")
    y = me // NX
    x = lax.rem(me, NX)

    def remote(src, dst, send_sem, recv_sem, target):
        return pltpu.make_async_remote_copy(
            src_ref=src,
            dst_ref=dst,
            send_sem=send_sem,
            recv_sem=recv_sem,
            device_id={"dap": target},
            device_id_type=MESH,
        )

    pairs = [
        (two, two_v),
        (map_t, map_v),
        (hom, hom_v),
        (win, win_v),
        (tpe, tpe_v),
        (wout, wout_v),
        (cwin, cwin_v),
        (cwout, cwout_v),
        (fac_t, fac_v),
    ]
    loads = [pltpu.make_async_copy(a, b, in_sem.at[n]) for n, (a, b) in enumerate(pairs)]
    for load in loads:
        load.start()
    names = ("two", "map", "hom", "win", "tpe", "wout", "cwin", "cwout", "fac")
    ready = dict(zip(names, loads))

    barrier = pltpu.get_barrier_semaphore()

    y_order = [1, 7, 2, 6, 3, 5, 4]
    x_order = [1, 3, 2]

    def at(dy, dx):
        return lax.rem(y + dy, NY) * NX + lax.rem(x + dx, NX)

    for dy, dx in [(k, 0) for k in reversed(y_order)] + [(0, k) for k in reversed(x_order)]:
        pl.semaphore_signal(barrier, inc=1, device_id={"dap": at(dy, dx)}, device_id_type=MESH)

    ready["two"].wait()
    ready["map"].wait()
    for i in range(4):
        pair_norm = standardized(two_v[i].astype(F32)).astype(BF16)
        b32[0, pl.ds(i, 8, stride=4), :] = dot_nt(map_v[...], pair_norm)
    bias_recv[me] = b32[0, 0:32, :].astype(BF16)

    pl.semaphore_wait(barrier, NY + NX - 2)

    bias_sends = []

    def send_bias(block, target):
        copy = remote(
            bias_recv.at[block],
            bias_recv.at[block],
            bs_sem.at[len(bias_sends)],
            br_sem.at[block],
            target,
        )
        copy.start()
        bias_sends.append(copy)

    def bias_arrived(block):
        remote(
            bias_recv.at[block], bias_recv.at[block], bs_sem.at[0], br_sem.at[block], me
        ).wait_recv()

    for k in reversed(y_order):
        send_bias(me, at(k, 0))
    for k in reversed(x_order):
        send_bias(me, at(0, k))

    ready["hom"].wait()
    ready["win"].wait()
    masks = head_masks()
    wide_masks = [jnp.concatenate([mask, mask], axis=1).astype(F32) for mask in masks]
    values = hom_v[...].reshape(512, 256).astype(F32)
    put(x32, 0, 512, values)
    normal = standardized(values)
    put(n32, 0, 512, normal)
    normal = normal.astype(BF16)
    k_s[...] = dot(normal, win_v[:, 256:512]).astype(BF16)
    v_s[...] = dot(normal, win_v[:, 512:768]).astype(BF16)

    def mixed(ref, group):
        return jnp.concatenate(
            [take(ref, s * 128 + group * 4 + i, 8, 16) for s in range(4) for i in range(4)],
            axis=0,
        )

    normal = jnp.concatenate([mixed(n32, group) for group in range(NX)], axis=0).astype(BF16)
    q_s[...] = dot(normal, win_v[:, 0:256]).astype(BF16).reshape(NX, 128, 256)
    gates = dot(normal, win_v[:, 768:1024]).astype(BF16).astype(F32)
    g_s[...] = jax.nn.sigmoid(gates).reshape(NX, 128, 256)
    for group in range(NX):
        xp[group] = mixed(x32, group)

    scale = LOG2E / math.sqrt(32)
    for s in range(4):
        rows = slice(s * 32, (s + 1) * 32)
        for g in range(2):
            lanes = slice(g * 128, (g + 1) * 128)
            query = jnp.concatenate(
                [q_s[c, rows, lanes] * mask for c in range(NX) for mask in masks], axis=0
            )
            scores = dot_nt(query, k_s[s * 128 : (s + 1) * 128, lanes]) * scale
            sc[:, g, s] = scores.reshape(NX, 128, 128)

    ready["tpe"].wait()
    w32[...] = tpe_v[...].astype(F32)
    bd[...] = jnp.zeros_like(bd)
    for e in range(32):
        piece = w32[pl.ds(e, 32, stride=32), :].astype(BF16)
        for i in range(4):
            bd[e * 128 + i * 32 : e * 128 + (i + 1) * 32, i * 128 : (i + 1) * 128] = piece

    for k in y_order:
        block = at(k, 0)
        bias_arrived(block)
        for m in reversed(x_order):
            send_bias(block, at(0, m))

    ready["wout"].wait()
    ones = jnp.ones((128, 128), BF16)
    for n, m in enumerate([0, 1, 2, 3]):
        column = lax.rem(x + m, NX)
        if m:
            for k in [0] + y_order:
                bias_arrived(at(k, m))
        for r in range(NY):
            b32[n, r * 32 : (r + 1) * 32, :] = bias_recv[r * NX + column].astype(F32) * LOG2E
        bias = [
            jnp.concatenate(
                [b32[n, pl.ds(g * 16 + i, 8, stride=32), :] for i in range(16)], axis=0
            )
            for g in range(2)
        ]
        parts = []
        for g in range(2):
            lanes = slice(g * 128, (g + 1) * 128)
            part = []
            for s in range(4):
                rows = slice(s * 32, (s + 1) * 32)
                scores = sc[column, g, s] + bias[g]
                highest = jnp.max(scores, axis=-1, keepdims=True)
                weights = jnp.exp2(scores - highest).astype(BF16)
                value = jnp.concatenate([v_s[s * 128 : (s + 1) * 128, lanes], ones], axis=1)
                both = dot(weights, value)
                both = sum(
                    both[h * 32 : (h + 1) * 32] * wide_masks[h] for h in range(4)
                )
                part.append(both[:, :128] / both[:, 128:] * g_s[column, rows, lanes])
            parts.append(jnp.concatenate(part, axis=0).astype(BF16))
        total = xp[column] + dot(jnp.concatenate(parts, axis=1), wout_v[...])
        for s in range(4):
            for i in range(4):
                start = s * 32 + i * 8
                for t in range(2):
                    m32[n, t, pl.ds(i * 4 + s, 8, stride=16), :] = total[
                        start : start + 8, t * 128 : (t + 1) * 128
                    ]
        for r in range(NY):
            rows = slice(r * 16, (r + 1) * 16)
            msend[r * NX + column] = jnp.concatenate(
                [m32[n, 0, rows, :], m32[n, 1, rows, :]], axis=1
            ).astype(BF16)
        if not m:
            mrecv[me] = msend[me]
        for k in list(reversed(y_order)) + ([] if m == 0 else [0]):
            target = at(k, m)
            remote(msend.at[target], mrecv.at[me], ms_sem, mr_sem.at[m], target).start()

    for copy in bias_sends:
        copy.wait_send()
    for name in ("cwin", "cwout", "fac"):
        ready[name].wait()

    for m in range(NX):
        column = lax.rem(x + NX - m, NX)
        count = NY - 1 if m == 0 else NY
        group = mrecv.at[pl.ds(0, count)]
        remote(group, group, ms_sem, mr_sem.at[m], me).wait_recv()
        values = jnp.concatenate([mrecv[r * NX + column] for r in range(NY)], axis=0).astype(F32)
        normal = standardized(values)
        base = pl.multiple_of(column * 32, 32)
        for r in range(NY):
            for i in range(4):
                start = r * 16 + i * 4
                for t in range(2):
                    lanes = slice(t * 128, (t + 1) * 128)
                    x32.at[t, pl.ds(i * 128 + base, 32), :][r * 4 : (r + 1) * 4, :] = values[
                        start : start + 4, lanes
                    ]
                    n32.at[t, pl.ds(i * 128 + base, 32), :][r * 4 : (r + 1) * 4, :] = normal[
                        start : start + 4, lanes
                    ]
    everything = msend.at[pl.ds(0, ND - 1)]
    remote(everything, everything, ms_sem, mr_sem.at[0], me).wait_send()

    sends = []
    done = []
    for half in range(2):
        pair = (half * 2, half * 2 + 1)
        rows = slice(half * 256, (half + 1) * 256)
        values = jnp.concatenate([x32[0, rows, :], x32[1, rows, :]], axis=1)
        normal = jnp.concatenate([n32[0, rows, :], n32[1, rows, :]], axis=1).astype(BF16)
        packed = [dot(normal, cwin_v[:, n * 256 : (n + 1) * 256]).astype(BF16) for n in range(4)]
        gated = []
        for n in range(2):
            parts = []
            for g in range(2):
                q, k, v, gate = [
                    part[n * 128 : (n + 1) * 128, g * 128 : (g + 1) * 128] for part in packed
                ]
                parts.append(attend(q, k, v, gate.astype(F32), masks))
            gated.append(jnp.concatenate(parts, axis=1))
        total = values + dot(jnp.concatenate(gated, axis=0), cwout_v[...])
        wide = total.astype(BF16).astype(F32)
        factors = dot_nt(fac_v[...], standardized(wide).astype(BF16)).astype(BF16)
        for n, r in enumerate(pair):
            l_all[x, r * 32 : (r + 1) * 32, :] = factors[:32, n * 128 : (n + 1) * 128]
            r_all[y, r * 32 : (r + 1) * 32, :] = factors[32:, n * 128 : (n + 1) * 128]
        rows = pl.ds(half * 64, 64)
        start = len(sends)
        for n, k in enumerate(reversed(y_order)):
            block = r_all.at[y, rows]
            sends.append(
                remote(block, block, rs_sem.at[half, n], rr_sem.at[half, y], at(k, 0))
            )
        for n, k in enumerate(reversed(x_order)):
            block = l_all.at[x, rows]
            sends.append(
                remote(block, block, ls_sem.at[half, n], lr_sem.at[half, x], at(0, k))
            )
        for copy in sends[start:]:
            copy.start()
        done.append(wide)
    for r in range(4):
        wide = done[r // 2]
        for c in range(NX):
            for d in range(NY):
                begin = (r % 2) * 128 + c * 32 + d * 4
                put(y32, (d * NX + c) * 16 + r, 4, wide[begin : begin + 4], stride=4)

    align_out[...] = jnp.concatenate([y32[0], y32[1]], axis=1).reshape(128, 4, 256).astype(BF16)

    def arrived(ref, peer, half, send_sem, recv_sem):
        block = ref.at[peer, pl.ds(half * 64, 64)]
        remote(block, block, send_sem.at[half, 0], recv_sem.at[half, peer], me).wait_recv()

    for half in range(2):
        for k in x_order:
            arrived(l_all, lax.rem(x + k, NX), half, ls_sem, lr_sem)
    left = l_all[...].reshape(NX * 128, 128)
    for half in range(2):
        for k in [0] + y_order:
            peer = lax.rem(y + k, NY)
            if k:
                arrived(r_all, peer, half, rs_sem, rr_sem)
            right = r_all[peer, half * 64 : (half + 1) * 64, :]
            product = dot_nt(right, left) * (1.0 / 128)
            for j in range(2):
                for e in range(0, 32, 8):
                    for n in range(NX):
                        start = e * 32 + (half * 2 + j) * 8 + peer
                        o32[n, pl.ds(start, 8, stride=32), :] = product[
                            j * 32 + e : j * 32 + e + 8, n * 128 : (n + 1) * 128
                        ]
    for e in range(32):
        ot[:, e * 128 : (e + 1) * 128] = jnp.concatenate(
            [o32[n, e * 32 : (e + 1) * 32, :] for n in range(NX)], axis=0
        ).astype(BF16)
    dsend[...] = dot(ot[...], bd[...]).astype(BF16).reshape(NX, 32, 512)
    for n, k in enumerate(reversed(x_order)):
        peer = lax.rem(x + k, NX)
        copy = remote(dsend.at[peer], drecv.at[x], ds_sem.at[n], dr_sem.at[x], at(0, k))
        copy.start()
        sends.append(copy)
    drecv[x] = dsend[x]
    for k in [0] + x_order:
        peer = lax.rem(x + k, NX)
        if k:
            block = drecv.at[peer]
            remote(block, block, ds_sem.at[0], dr_sem.at[peer], me).wait_recv()
        block = drecv[peer].astype(F32)
        for i in range(4):
            for j in range(4):
                f32s[pl.ds(i * 128 + peer * 4 + j, 8, stride=16), :] = block[
                    j * 8 : (j + 1) * 8, i * 128 : (i + 1) * 128
                ]
    pair_out[...] = (f32s[...] + two_v[...].reshape(512, 128).astype(F32)).astype(BF16).reshape(4, 128, 128)
    for copy in sends:
        copy.wait_send()


def write_out(align, pair, align_out, pair_out, sem):
    copies = [
        pltpu.make_async_copy(align, align_out, sem.at[0]),
        pltpu.make_async_copy(pair, pair_out, sem.at[1]),
    ]
    for copy in copies:
        copy.start()
    for copy in copies:
        copy.wait()


def per_device(hom, two, offset_map, win, wout, cwin, cwout, factors, tpe):
    operands = (hom, two, offset_map.T, win, wout, cwin, cwout, factors.T, tpe)
    operands = tuple(pltpu.with_memory_space_constraint(a, pltpu.HBM) for a in operands)
    dma = pltpu.SemaphoreType.DMA
    vm = pltpu.VMEM
    scratch = [vm(a.shape, BF16) for a in operands] + [
        vm((2, 512, 128), F32),
        vm((2, 512, 128), F32),
        vm((NX, 128, 256), BF16),
        vm((512, 256), BF16),
        vm((512, 256), BF16),
        vm((NX, 128, 256), F32),
        vm((NX, 2, 4, 128, 128), F32),
        vm((NX, 128, 256), F32),
        vm((NX, 256, 128), F32),
        vm((ND, 32, 128), BF16),
        vm((NX, 2, 128, 128), F32),
        vm((ND, 16, 256), BF16),
        vm((ND, 16, 256), BF16),
        vm((2, 512, 128), F32),
        vm((NX, 128, 128), BF16),
        vm((NY, 128, 128), BF16),
        vm((NX, NY * 128, 128), F32),
        vm((128, 4096), BF16),
        vm((1024, 128), F32),
        vm((4096, 512), BF16),
        vm((NX, 32, 512), BF16),
        vm((NX, 32, 512), BF16),
        vm((512, 128), F32),
        dma((9,)),
        dma((31,)),
        dma((ND,)),
        dma,
        dma((NX,)),
        dma((2, 3)),
        dma((2, NX)),
        dma((2, 7)),
        dma((2, NY)),
        dma((3,)),
        dma((NX,)),
    ]
    hbm = pl.BlockSpec(memory_space=pl.ANY)
    align, pair = pl.pallas_call(
        kernel,
        out_shape=(
            jax.ShapeDtypeStruct((128, 4, 256), BF16),
            jax.ShapeDtypeStruct((4, 128, 128), BF16),
        ),
        in_specs=[hbm] * len(operands),
        out_specs=(pl.BlockSpec(memory_space=pltpu.VMEM),) * 2,
        scratch_shapes=scratch,
        compiler_params=pltpu.CompilerParams(collective_id=0, has_side_effects=True, vmem_limit_bytes=40 * 2**20),
    )(*operands)
    return pl.pallas_call(
        write_out,
        out_shape=(
            jax.ShapeDtypeStruct((128, 4, 256), BF16),
            jax.ShapeDtypeStruct((4, 128, 128), BF16),
        ),
        in_specs=[pl.BlockSpec(memory_space=pltpu.VMEM)] * 2,
        out_specs=(hbm, hbm),
        scratch_shapes=[dma((2,))],
        compiler_params=pltpu.CompilerParams(vmem_limit_bytes=40 * 2**20),
    )(align, pair)


def solution(mesh):
    split = P(("crop", "dap"), None, None)
    return jax.shard_map(
        per_device,
        mesh=mesh,
        in_specs=(split, split) + (P(),) * 7,
        out_specs=(P("crop", "dap", None), split),
        check_vma=False,
    )
```

```python
import math

import jax
import jax.numpy as jnp
from jax import lax
from jax.experimental import pallas as pl
from jax.experimental.pallas import tpu as pltpu
from jax.sharding import PartitionSpec as P

EPSILON = 1e-05
MESH = pl.DeviceIdType.MESH
F32 = jnp.float32
BF16 = jnp.bfloat16
LOG2E = math.log2(math.e)
NX = 4
NY = 8
ND = NX * NY
NT = (((1,), (1,)), ((), ()))


def standardized(values):
    center = values - jnp.mean(values, axis=-1, keepdims=True)
    spread = jnp.mean(center * center, axis=-1, keepdims=True)
    return center * lax.rsqrt(spread + EPSILON)


def dot(a, b):
    return jnp.dot(a, b, preferred_element_type=F32)


def dot_nt(a, b):
    return lax.dot_general(a, b, NT, preferred_element_type=F32)


def put(ref, start, size, value, stride=1):
    rows = pl.ds(start, size, stride=stride) if stride > 1 else pl.ds(start, size)
    for t in range(value.shape[1] // 128):
        ref[t, rows, :] = value[:, t * 128 : (t + 1) * 128]


def take(ref, start, size, stride):
    rows = pl.ds(start, size, stride=stride)
    return jnp.concatenate([ref[t, rows, :] for t in range(ref.shape[0])], axis=1)


def head_masks():
    lane = lax.broadcasted_iota(jnp.int32, (1, 128), 1)
    return [jnp.where(lane // 32 == h, 1.0, 0.0).astype(BF16) for h in range(4)]


def attend(q, k, v, gate, masks):
    scale = LOG2E / math.sqrt(32)
    rows = q.shape[0]
    query = jnp.concatenate([q * mask for mask in masks], axis=0)
    scores = dot_nt(query, k) * scale
    highest = jnp.max(scores, axis=-1, keepdims=True)
    stacked = jnp.exp2(scores - highest).astype(BF16)
    weights = [stacked[h * rows : (h + 1) * rows] for h in range(4)]
    values = [
        jnp.concatenate([v * mask, jnp.broadcast_to(mask, v.shape)], axis=1) for mask in masks
    ]
    both = dot(jnp.concatenate(weights, axis=1), jnp.concatenate(values, axis=0))
    return (jax.nn.sigmoid(gate) * (both[:, :128] / both[:, 128:])).astype(BF16)


def kernel(
    hom,
    two,
    map_t,
    win,
    wout,
    cwin,
    cwout,
    fac_t,
    tpe,
    align_out,
    pair_out,
    hom_v,
    two_v,
    map_v,
    win_v,
    wout_v,
    cwin_v,
    cwout_v,
    fac_v,
    tpe_v,
    x32,
    n32,
    q_s,
    k_s,
    v_s,
    g_s,
    sc,
    xp,
    b32,
    bias_recv,
    m32,
    msend,
    mrecv,
    y32,
    l_all,
    r_all,
    o32,
    ot,
    w32,
    bd,
    dsend,
    drecv,
    f32s,
    in_sem,
    bs_sem,
    br_sem,
    ms_sem,
    mr_sem,
    ls_sem,
    lr_sem,
    rs_sem,
    rr_sem,
    ds_sem,
    dr_sem,
):
    me = lax.axis_index("dap")
    y = me // NX
    x = lax.rem(me, NX)

    def remote(src, dst, send_sem, recv_sem, target):
        return pltpu.make_async_remote_copy(
            src_ref=src,
            dst_ref=dst,
            send_sem=send_sem,
            recv_sem=recv_sem,
            device_id={"dap": target},
            device_id_type=MESH,
        )

    pairs = [
        (two, two_v),
        (map_t, map_v),
        (hom, hom_v),
        (win, win_v),
        (tpe, tpe_v),
        (wout, wout_v),
        (cwin, cwin_v),
        (cwout, cwout_v),
        (fac_t, fac_v),
    ]
    loads = [pltpu.make_async_copy(a, b, in_sem.at[n]) for n, (a, b) in enumerate(pairs)]
    for load in loads:
        load.start()
    names = ("two", "map", "hom", "win", "tpe", "wout", "cwin", "cwout", "fac")
    ready = dict(zip(names, loads))

    barrier = pltpu.get_barrier_semaphore()

    y_order = [1, 7, 2, 6, 3, 5, 4]
    x_order = [1, 3, 2]

    def at(dy, dx):
        return lax.rem(y + dy, NY) * NX + lax.rem(x + dx, NX)

    for dy, dx in [(k, 0) for k in reversed(y_order)] + [(0, k) for k in reversed(x_order)]:
        pl.semaphore_signal(barrier, inc=1, device_id={"dap": at(dy, dx)}, device_id_type=MESH)

    ready["two"].wait()
    ready["map"].wait()
    for i in range(4):
        pair_norm = standardized(two_v[i].astype(F32)).astype(BF16)
        b32[0, pl.ds(i, 8, stride=4), :] = dot_nt(map_v[...], pair_norm)
    bias_recv[me] = b32[0, 0:32, :].astype(BF16)

    pl.semaphore_wait(barrier, NY + NX - 2)

    bias_sends = []

    def send_bias(block, target):
        copy = remote(
            bias_recv.at[block],
            bias_recv.at[block],
            bs_sem.at[len(bias_sends)],
            br_sem.at[block],
            target,
        )
        copy.start()
        bias_sends.append(copy)

    def bias_arrived(block):
        remote(
            bias_recv.at[block], bias_recv.at[block], bs_sem.at[0], br_sem.at[block], me
        ).wait_recv()

    for k in reversed(y_order):
        send_bias(me, at(k, 0))
    for k in reversed(x_order):
        send_bias(me, at(0, k))

    ready["hom"].wait()
    ready["win"].wait()
    masks = head_masks()
    wide_masks = [jnp.concatenate([mask, mask], axis=1).astype(F32) for mask in masks]
    values = hom_v[...].reshape(512, 256).astype(F32)
    put(x32, 0, 512, values)
    normal = standardized(values)
    put(n32, 0, 512, normal)
    normal = normal.astype(BF16)
    k_s[...] = dot(normal, win_v[:, 256:512]).astype(BF16)
    v_s[...] = dot(normal, win_v[:, 512:768]).astype(BF16)

    def mixed(ref, group):
        return jnp.concatenate(
            [take(ref, s * 128 + group * 4 + i, 8, 16) for s in range(4) for i in range(4)],
            axis=0,
        )

    normal = jnp.concatenate([mixed(n32, group) for group in range(NX)], axis=0).astype(BF16)
    q_s[...] = dot(normal, win_v[:, 0:256]).astype(BF16).reshape(NX, 128, 256)
    gates = dot(normal, win_v[:, 768:1024]).astype(BF16).astype(F32)
    g_s[...] = jax.nn.sigmoid(gates).reshape(NX, 128, 256)
    for group in range(NX):
        xp[group] = mixed(x32, group)

    scale = LOG2E / math.sqrt(32)
    for s in range(4):
        rows = slice(s * 32, (s + 1) * 32)
        for g in range(2):
            lanes = slice(g * 128, (g + 1) * 128)
            query = jnp.concatenate(
                [q_s[c, rows, lanes] * mask for c in range(NX) for mask in masks], axis=0
            )
            scores = dot_nt(query, k_s[s * 128 : (s + 1) * 128, lanes]) * scale
            sc[:, g, s] = scores.reshape(NX, 128, 128)

    ready["tpe"].wait()
    w32[...] = tpe_v[...].astype(F32)
    bd[...] = jnp.zeros_like(bd)
    for e in range(32):
        piece = w32[pl.ds(e, 32, stride=32), :].astype(BF16)
        for i in range(4):
            bd[e * 128 + i * 32 : e * 128 + (i + 1) * 32, i * 128 : (i + 1) * 128] = piece

    for k in y_order:
        block = at(k, 0)
        bias_arrived(block)
        for m in reversed(x_order):
            send_bias(block, at(0, m))

    ready["wout"].wait()
    ones = jnp.ones((128, 128), BF16)
    for n, m in enumerate([0, 1, 2, 3]):
        column = lax.rem(x + m, NX)
        if m:
            for k in [0] + y_order:
                bias_arrived(at(k, m))
        for r in range(NY):
            b32[n, r * 32 : (r + 1) * 32, :] = bias_recv[r * NX + column].astype(F32) * LOG2E
        bias = [
            jnp.concatenate(
                [b32[n, pl.ds(g * 16 + i, 8, stride=32), :] for i in range(16)], axis=0
            )
            for g in range(2)
        ]
        parts = []
        for g in range(2):
            lanes = slice(g * 128, (g + 1) * 128)
            part = []
            for s in range(4):
                rows = slice(s * 32, (s + 1) * 32)
                scores = sc[column, g, s] + bias[g]
                highest = jnp.max(scores, axis=-1, keepdims=True)
                weights = jnp.exp2(scores - highest).astype(BF16)
                value = jnp.concatenate([v_s[s * 128 : (s + 1) * 128, lanes], ones], axis=1)
                both = dot(weights, value)
                both = sum(
                    both[h * 32 : (h + 1) * 32] * wide_masks[h] for h in range(4)
                )
                part.append(both[:, :128] / both[:, 128:] * g_s[column, rows, lanes])
            parts.append(jnp.concatenate(part, axis=0).astype(BF16))
        total = xp[column] + dot(jnp.concatenate(parts, axis=1), wout_v[...])
        for s in range(4):
            for i in range(4):
                start = s * 32 + i * 8
                for t in range(2):
                    m32[n, t, pl.ds(i * 4 + s, 8, stride=16), :] = total[
                        start : start + 8, t * 128 : (t + 1) * 128
                    ]
        for r in range(NY):
            rows = slice(r * 16, (r + 1) * 16)
            msend[r * NX + column] = jnp.concatenate(
                [m32[n, 0, rows, :], m32[n, 1, rows, :]], axis=1
            ).astype(BF16)
        if not m:
            mrecv[me] = msend[me]
        for k in list(reversed(y_order)) + ([] if m == 0 else [0]):
            target = at(k, m)
            remote(msend.at[target], mrecv.at[me], ms_sem, mr_sem.at[m], target).start()

    for copy in bias_sends:
        copy.wait_send()
    for name in ("cwin", "cwout", "fac"):
        ready[name].wait()

    for m in range(NX):
        column = lax.rem(x + NX - m, NX)
        count = NY - 1 if m == 0 else NY
        group = mrecv.at[pl.ds(0, count)]
        remote(group, group, ms_sem, mr_sem.at[m], me).wait_recv()
        values = jnp.concatenate([mrecv[r * NX + column] for r in range(NY)], axis=0).astype(F32)
        normal = standardized(values)
        base = pl.multiple_of(column * 32, 32)
        for r in range(NY):
            for i in range(4):
                start = r * 16 + i * 4
                for t in range(2):
                    lanes = slice(t * 128, (t + 1) * 128)
                    x32.at[t, pl.ds(i * 128 + base, 32), :][r * 4 : (r + 1) * 4, :] = values[
                        start : start + 4, lanes
                    ]
                    n32.at[t, pl.ds(i * 128 + base, 32), :][r * 4 : (r + 1) * 4, :] = normal[
                        start : start + 4, lanes
                    ]
    everything = msend.at[pl.ds(0, ND - 1)]
    remote(everything, everything, ms_sem, mr_sem.at[0], me).wait_send()

    sends = []
    done = []
    for half in range(2):
        pair = (half * 2, half * 2 + 1)
        rows = slice(half * 256, (half + 1) * 256)
        values = jnp.concatenate([x32[0, rows, :], x32[1, rows, :]], axis=1)
        normal = jnp.concatenate([n32[0, rows, :], n32[1, rows, :]], axis=1).astype(BF16)
        packed = [dot(normal, cwin_v[:, n * 256 : (n + 1) * 256]).astype(BF16) for n in range(4)]
        gated = []
        for n in range(2):
            parts = []
            for g in range(2):
                q, k, v, gate = [
                    part[n * 128 : (n + 1) * 128, g * 128 : (g + 1) * 128] for part in packed
                ]
                parts.append(attend(q, k, v, gate.astype(F32), masks))
            gated.append(jnp.concatenate(parts, axis=1))
        total = values + dot(jnp.concatenate(gated, axis=0), cwout_v[...])
        wide = total.astype(BF16).astype(F32)
        factors = dot_nt(fac_v[...], standardized(wide).astype(BF16)).astype(BF16)
        for n, r in enumerate(pair):
            l_all[x, r * 32 : (r + 1) * 32, :] = factors[:32, n * 128 : (n + 1) * 128]
            r_all[y, r * 32 : (r + 1) * 32, :] = factors[32:, n * 128 : (n + 1) * 128]
        rows = pl.ds(half * 64, 64)
        start = len(sends)
        for n, k in enumerate(reversed(y_order)):
            block = r_all.at[y, rows]
            sends.append(
                remote(block, block, rs_sem.at[half, n], rr_sem.at[half, y], at(k, 0))
            )
        for n, k in enumerate(reversed(x_order)):
            block = l_all.at[x, rows]
            sends.append(
                remote(block, block, ls_sem.at[half, n], lr_sem.at[half, x], at(0, k))
            )
        for copy in sends[start:]:
            copy.start()
        done.append(wide)
    for r in range(4):
        wide = done[r // 2]
        for c in range(NX):
            for d in range(NY):
                begin = (r % 2) * 128 + c * 32 + d * 4
                put(y32, (d * NX + c) * 16 + r, 4, wide[begin : begin + 4], stride=4)

    align_out[...] = jnp.concatenate([y32[0], y32[1]], axis=1).reshape(128, 4, 256).astype(BF16)

    def arrived(ref, peer, half, send_sem, recv_sem):
        block = ref.at[peer, pl.ds(half * 64, 64)]
        remote(block, block, send_sem.at[half, 0], recv_sem.at[half, peer], me).wait_recv()

    for half in range(2):
        for k in x_order:
            arrived(l_all, lax.rem(x + k, NX), half, ls_sem, lr_sem)
    left = l_all[...].reshape(NX * 128, 128)
    for half in range(2):
        for k in [0] + y_order:
            peer = lax.rem(y + k, NY)
            if k:
                arrived(r_all, peer, half, rs_sem, rr_sem)
            right = r_all[peer, half * 64 : (half + 1) * 64, :]
            product = dot_nt(right, left) * (1.0 / 128)
            for j in range(2):
                for e in range(0, 32, 8):
                    for n in range(NX):
                        start = e * 32 + (half * 2 + j) * 8 + peer
                        o32[n, pl.ds(start, 8, stride=32), :] = product[
                            j * 32 + e : j * 32 + e + 8, n * 128 : (n + 1) * 128
                        ]
    for e in range(32):
        ot[:, e * 128 : (e + 1) * 128] = jnp.concatenate(
            [o32[n, e * 32 : (e + 1) * 32, :] for n in range(NX)], axis=0
        ).astype(BF16)
    dsend[...] = dot(ot[...], bd[...]).astype(BF16).reshape(NX, 32, 512)
    for n, k in enumerate(reversed(x_order)):
        peer = lax.rem(x + k, NX)
        copy = remote(dsend.at[peer], drecv.at[x], ds_sem.at[n], dr_sem.at[x], at(0, k))
        copy.start()
        sends.append(copy)
    drecv[x] = dsend[x]
    for k in [0] + x_order:
        peer = lax.rem(x + k, NX)
        if k:
            block = drecv.at[peer]
            remote(block, block, ds_sem.at[0], dr_sem.at[peer], me).wait_recv()
        block = drecv[peer].astype(F32)
        for i in range(4):
            for j in range(4):
                f32s[pl.ds(i * 128 + peer * 4 + j, 8, stride=16), :] = block[
                    j * 8 : (j + 1) * 8, i * 128 : (i + 1) * 128
                ]
    pair_out[...] = (f32s[...] + two_v[...].reshape(512, 128).astype(F32)).astype(BF16).reshape(4, 128, 128)
    for copy in sends:
        copy.wait_send()


def write_out(align, pair, align_out, pair_out, sem):
    copies = [
        pltpu.make_async_copy(align, align_out, sem.at[0]),
        pltpu.make_async_copy(pair, pair_out, sem.at[1]),
    ]
    for copy in copies:
        copy.start()
    for copy in copies:
        copy.wait()


def per_device(hom, two, offset_map, win, wout, cwin, cwout, factors, tpe):
    operands = (hom, two, offset_map.T, win, wout, cwin, cwout, factors.T, tpe)
    operands = tuple(pltpu.with_memory_space_constraint(a, pltpu.HBM) for a in operands)
    dma = pltpu.SemaphoreType.DMA
    vm = pltpu.VMEM
    scratch = [vm(a.shape, BF16) for a in operands] + [
        vm((2, 512, 128), F32),
        vm((2, 512, 128), F32),
        vm((NX, 128, 256), BF16),
        vm((512, 256), BF16),
        vm((512, 256), BF16),
        vm((NX, 128, 256), F32),
        vm((NX, 2, 4, 128, 128), F32),
        vm((NX, 128, 256), F32),
        vm((NX, 256, 128), F32),
        vm((ND, 32, 128), BF16),
        vm((NX, 2, 128, 128), F32),
        vm((ND, 16, 256), BF16),
        vm((ND, 16, 256), BF16),
        vm((2, 512, 128), F32),
        vm((NX, 128, 128), BF16),
        vm((NY, 128, 128), BF16),
        vm((NX, NY * 128, 128), F32),
        vm((128, 4096), BF16),
        vm((1024, 128), F32),
        vm((4096, 512), BF16),
        vm((NX, 32, 512), BF16),
        vm((NX, 32, 512), BF16),
        vm((512, 128), F32),
        dma((9,)),
        dma((31,)),
        dma((ND,)),
        dma,
        dma((NX,)),
        dma((2, 3)),
        dma((2, NX)),
        dma((2, 7)),
        dma((2, NY)),
        dma((3,)),
        dma((NX,)),
    ]
    hbm = pl.BlockSpec(memory_space=pl.ANY)
    align, pair = pl.pallas_call(
        kernel,
        out_shape=(
            jax.ShapeDtypeStruct((128, 4, 256), BF16),
            jax.ShapeDtypeStruct((4, 128, 128), BF16),
        ),
        in_specs=[hbm] * len(operands),
        out_specs=(pl.BlockSpec(memory_space=pltpu.VMEM),) * 2,
        scratch_shapes=scratch,
        compiler_params=pltpu.CompilerParams(collective_id=0, has_side_effects=True, vmem_limit_bytes=40 * 2**20),
    )(*operands)
    return pl.pallas_call(
        write_out,
        out_shape=(
            jax.ShapeDtypeStruct((128, 4, 256), BF16),
            jax.ShapeDtypeStruct((4, 128, 128), BF16),
        ),
        in_specs=[pl.BlockSpec(memory_space=pltpu.VMEM)] * 2,
        out_specs=(hbm, hbm),
        scratch_shapes=[dma((2,))],
        compiler_params=pltpu.CompilerParams(vmem_limit_bytes=40 * 2**20),
    )(align, pair)


def solution(mesh):
    split = P(("crop", "dap"), None, None)
    return jax.shard_map(
        per_device,
        mesh=mesh,
        in_specs=(split, split) + (P(),) * 7,
        out_specs=(P("crop", "dap", None), split),
        check_vma=False,
    )
```
